32 devices in a mesh: wide: 8 (over y, x, core), narrow: 4 (over z).
Axes of the slice: x: 2, y: 2, z: 4, core: 2. Of those that a mesh axis runs over, the one named last changes fastest.
Arguments:
- hamiltonian_tiles: float32 [12288, 6144], P('wide', 'narrow'), may hold values from -0.0546875 to 0.0546875
- row_columns: int32 [8, 4], P('wide'), may hold values from 0 to 7, as said below
- start_vectors: float32 [12288, 128], P(('wide', 'narrow')), may hold values from -60 to 60
Outputs:
- new_vectors: float32 [12288, 128], P(('wide', 'narrow'))
The draws below stay inside these ranges and needn't reach their ends.
Inputs may be any that keep to these rules, and one draw needn't show every extreme that they name: For block row r = w + j // 4, row_columns[w, j] = (r + d) mod 8, with d = 0 where j % 4 = 0 and, for the other tiles of that block row, distinct d between 1 and 7; a block's mirror may also be stored.
All inputs are finite; a program needn't handle non-finite values.
Results may differ from the reference program's by a relative error of at most 0.0003.
Values sent between devices are 32-bit elements; how exact they have to be, the bound alone decides.
A program may use at most 64 MiB of HBM per device.

```python
import jax
import jax.numpy as jnp
from jax import lax

B = 1536
K = 128
ITERS = 2
NS_STEPS = 5
TILES_ROW = 4
NB = 8
N_WIDE = 8
N_NARROW = 4


def draw_row_columns(key, part):
    rows_group = N_NARROW // TILES_ROW
    blocks = N_WIDE * rows_group
    half = blocks // 2
    count = blocks - 2
    candidates = jnp.arange(count, dtype=jnp.int32) + 1
    scores = jax.random.randint(jax.random.fold_in(key, 11), (blocks, count), 0, 1048576)
    scores = scores * blocks + jnp.arange(count, dtype=jnp.int32)[None, :]
    scores = jnp.where(candidates[None, :] == half, 2000000000, scores)
    order = jnp.argsort(scores, axis=1).astype(jnp.int32)
    randoms = order[:, :TILES_ROW - 3] + 1
    fixed = jnp.concatenate([jnp.zeros((blocks, 1), jnp.int32), jnp.full((blocks, 1), half, jnp.int32), jnp.full((blocks, 1), blocks - 1, jnp.int32)], axis=1)
    offsets = jnp.concatenate([fixed, randoms], axis=1)
    rows = jnp.arange(blocks, dtype=jnp.int32)[:, None]
    return ((rows + offsets) % blocks).reshape(N_WIDE, N_NARROW).astype(jnp.int32)


def draw_start_vectors(key, part):
    column_key = jax.random.fold_in(key, 21)
    entry_key = jax.random.fold_in(key, 22)
    column_scale = 10.0 ** jax.random.uniform(column_key, (1, K), jnp.float32, 0.0, 1.0)
    entries = jax.random.normal(entry_key, (NB * B, K), jnp.float32)
    values = entries * column_scale
    return jnp.clip(values, -60.0, 60.0).astype(jnp.float32)


def level_of(own_key, shape, cuts, least, largest):
    def one(position, blocks):
        draws = jax.random.uniform(jax.random.fold_in(jax.random.fold_in(own_key, 6), position), (blocks,), jnp.float32, least / len(cuts), largest / len(cuts))
        return jnp.repeat(jnp.exp(draws), shape[position] // blocks).reshape((-1,) + (1,) * (len(shape) - position - 1))

    loudness = one(*cuts[0])
    for cut in cuts[1:]:
        loudness = loudness * one(*cut)
    return loudness


def bell_draw(rng, dims, deviation, bound, cuts=(), kind=jnp.bfloat16):
    drawn = jax.random.normal(rng, dims, jnp.float32) * deviation
    if len(cuts) > 0:
        drawn = level_of(rng, dims, cuts, -0.22, 0.18) * drawn
    return jnp.clip(drawn, min=-bound, max=bound).astype(kind)


def setup_inputs(seed: int = 0) -> dict:
    seeds = jax.random.split(jax.random.key(seed), 4)
    return {
        "hamiltonian_tiles": bell_draw(seeds[0], (N_WIDE * B, N_NARROW * B), (2 * B * TILES_ROW) ** -0.5, 0.0546875, ((0, 8), (1, 4)), jnp.float32),
        "row_columns": draw_row_columns(jax.random.fold_in(seeds[3], 71), 0),
        "start_vectors": draw_start_vectors(jax.random.fold_in(seeds[3], 71), 0),
    }


def apply_hamiltonian(tiles, columns, vectors):
    rows_group = N_NARROW // TILES_ROW
    blocks = vectors.reshape(NB, B, K)
    grouped = tiles.reshape(N_WIDE, B, N_NARROW, B)
    owned = blocks.reshape(N_WIDE, rows_group, B, K)

    def one_group(carry, inputs):
        group_tiles, group_cols, own_blocks = inputs
        quad = group_tiles.reshape(B, rows_group, TILES_ROW, B)
        cols = group_cols.astype(jnp.int32).reshape(rows_group, TILES_ROW)
        column_blocks = blocks[cols]
        direct = jnp.einsum('iqtj,qtjk->qik', quad, column_blocks, precision=lax.Precision.HIGHEST)
        transposed = jnp.einsum('iqtj,qik->qtjk', quad, own_blocks, precision=lax.Precision.HIGHEST)
        carry = carry.at[cols.reshape(N_NARROW)].add(transposed.reshape(N_NARROW, B, K))
        return (carry, direct)
    zeros = jnp.zeros((NB, B, K), jnp.float32)
    moved, direct_rows = lax.scan(one_group, zeros, (grouped, columns, owned))
    return (direct_rows.reshape(NB, B, K) + moved).reshape(NB * B, K)

def orthonormalize(product, gram):
    identity = jnp.eye(K, dtype=jnp.float32)
    scale = jnp.sqrt(jnp.sum(gram * gram) + 1e-06)
    current = gram / scale
    inverse = identity
    for repeat in range(NS_STEPS):
        middle = 1.5 * identity - 0.5 * jnp.dot(inverse, current, precision=lax.Precision.HIGHEST)
        current = jnp.dot(current, middle, precision=lax.Precision.HIGHEST)
        inverse = jnp.dot(middle, inverse, precision=lax.Precision.HIGHEST)
    return jnp.dot(product, inverse, precision=lax.Precision.HIGHEST) * jnp.sqrt(NB * B / scale)

def reference(hamiltonian_tiles, row_columns, start_vectors):
    vectors = start_vectors
    for repeat in range(ITERS):
        product = apply_hamiltonian(hamiltonian_tiles, row_columns, vectors)
        gram = jnp.dot(product.T, product, precision=lax.Precision.HIGHEST)
        vectors = orthonormalize(product, gram)
    return vectors
```

```python
import functools

import jax
import jax.numpy as jnp
from jax import lax
from jax.experimental import pallas as pl
from jax.experimental.pallas import tpu as pltpu
from jax.sharding import PartitionSpec as P

ITERS = 2
NS_STEPS = 5
HIGHEST = lax.Precision.HIGHEST
MESH = pl.DeviceIdType.MESH
LOAD_CHUNKS = 6
ORDER = (
    7, 8, 9, 0, 6, 23, 15, 1, 134, 11, 24, 16, 25, 2, 17, 3, 35, 27, 28, 22, 14, 44, 43, 36,
    19, 4, 12, 5, 39, 20, 26, 10, 13, 21, 18, 55, 57, 59, 29, 31, 56, 50, 51, 52, 67, 54, 53, 40,
    32, 60, 62, 61, 45, 30, 34, 37, 65, 42, 48, 46, 38, 66, 33, 68, 47, 87, 41, 69, 75, 86, 63, 49,
    89, 95, 90, 103, 91, 94, 105, 77, 102, 70, 76, 74, 88, 107, 58, 99, 71, 80, 64, 72, 73, 81, 78, 79,
    82, 115, 93, 106, 117, 104, 114, 84, 122, 83, 97, 109, 98, 119, 116, 111, 92, 118, 96, 108, 123, 101, 100, 121,
    124, 120, 110, 125, 85, 127, 113, 112, 136, 126, 135, 129, 138, 128, 137, 130, 152, 144, 132, 151, 143, 131, 154, 153,
    133, 156, 172, 146, 163, 164, 243, 145, 155, 167, 148, 141, 168, 166, 165, 147, 196, 171, 170, 139, 140, 158, 198, 150,
    244, 149, 142, 179, 183, 180, 169, 157, 181, 182, 159, 160, 189, 191, 184, 185, 174, 162, 161, 190, 175, 176, 194, 218,
    215, 178, 177, 195, 173, 188, 217, 200, 234, 216, 193, 231, 192, 219, 199, 201, 223, 187, 203, 208, 233, 197, 186, 202,
    245, 209, 210, 227, 207, 204, 235, 205, 206, 211, 251, 226, 224, 254, 222, 232, 220, 213, 259, 238, 228, 221, 225, 253,
    212, 255, 236, 237, 239, 252, 229, 258, 230, 261, 240, 246, 247, 257, 260, 248, 249, 250, 256, 241, 262, 214, 263, 267,
    242, 265, 269, 264, 268, 266, 270, 271, 272, 273, 274, 275, 276, 277, 278,
)


def flip(x, mask):
    bit = 1
    while bit <= mask:
        if mask & bit:
            x = x + bit * (1 - 2 * ((x // bit) % 2))
        bit *= 2
    return x


def bits_of(count):
    bits = count.bit_length() - 1
    assert count == 1 << bits
    return bits


def lowest(q, bits):
    return bits if q == 0 else (q & -q).bit_length() - 1


def position(relative, order):
    return sum(((relative >> bit) & 1) << place for place, bit in enumerate(order))


class Routes:
    def __init__(self, wide, narrow):
        self.wide, self.narrow = wide, narrow
        self.wbits, self.nbits = bits_of(wide), bits_of(narrow)
        self.cuts = max(1, 4 * 4 // narrow)
        upper = list(range(1, self.wbits))
        self.lines = [upper, upper[::-1]]
        self.whole = []
        self.half = []
        for q in range(narrow):
            for c in range(self.cuts):
                if self.paired(q, c):
                    if q % 2 == 0:
                        self.whole.append((q, c))
                else:
                    self.half.append((q, c))

    def side(self, q, c):
        return (q + c) % 2

    def paired(self, q, c):
        return q < 2

    def order(self, q, c):
        line = self.lines[self.side(q, c)]
        return line + [0] if self.paired(q, c) else line[:-1] + [0]

    def last(self, q, c):
        return self.lines[self.side(q, c)][-1]

    def children(self, q):
        return [q | (1 << b) for b in range(lowest(q, self.nbits) - 1, -1, -1)]


def steps_of(routes):
    quarters, cuts = range(routes.narrow), range(routes.cuts)
    steps = [("load", i) for i in range(LOAD_CHUNKS)]
    for it in range(ITERS):
        if it > 0:
            steps.append(("turn", it))
        for q in quarters:
            for c in cuts:
                steps.append(("have", it, q, c))
        for level in range(1, routes.wbits):
            for q in quarters:
                for c in cuts:
                    paired = routes.paired(q, c)
                    if paired and q % 2 == 1:
                        continue
                    if level < len(routes.order(q, c)):
                        steps.append(("step", it, q, c, level))
        for q in quarters:
            for c in cuts:
                if not (routes.paired(q, c) and q % 2 == 1):
                    steps.append(("pick", it, q, c))
        for q in quarters[::-1]:
            steps.append(("trans", it, q))
            for c in cuts:
                if not (routes.paired(q, c) and q % 2 == 0):
                    steps.append(("pass", it, q, c))
        for q in quarters:
            for c in cuts:
                steps.append(("column", it, q, c))
        for q in quarters[::-1]:
            steps.append(("direct", it, q))
        for q in quarters[::-1]:
            for c in cuts:
                if not (routes.paired(q, c) and q % 2 == 1):
                    steps.append(("put", it, q, c))
        for level in range(routes.wbits - 1, 0, -1):
            for q in quarters[::-1]:
                for c in cuts:
                    if routes.paired(q, c) and q % 2 == 1:
                        continue
                    if level < len(routes.order(q, c)):
                        steps.append(("down", it, q, c, level))
        if it > 0:
            steps.append(("spread", it - 1))
            steps.append(("sum", it - 1))
            steps.append(("all", it - 1))
            steps += [("root", it - 1, repeat) for repeat in range(NS_STEPS)]
        for q in quarters[::-1]:
            for c in cuts:
                steps.append(("merge", it, q, c))
        for c in cuts:
            steps.append(("gram", it, c))
    steps.append(("spread", ITERS - 1))
    steps.append(("sum", ITERS - 1))
    steps.append(("all", ITERS - 1))
    steps += [("root", ITERS - 1, repeat) for repeat in range(NS_STEPS)]
    return steps


def sends_of(routes):
    count = 2
    pieces = routes.narrow * routes.cuts
    for it in range(ITERS):
        count += 2 * (routes.narrow - 1) * routes.cuts
        count += 2 * len(routes.whole) * (routes.wbits + 1)
        count += 2 * len(routes.half) * routes.wbits
        count += 2 * (routes.wide - 1) + routes.narrow - 1
    return count


def split(x):
    high = x.astype(jnp.bfloat16)
    low = (x - high.astype(jnp.float32)).astype(jnp.bfloat16)
    return high, low


def tree_sum(values):
    while len(values) > 1:
        values = [a + b for a, b in zip(values[::2], values[1::2])]
    return values[0]


def kernel(routes, sequence, slots, row_columns, tile_hbm, start, out, stage, tile_hi, tile_lo, turn_hi, turn_lo,
           rows_right, columns_right, trans, direct, whole_in, half_in, mate_rows, picks, picked, choices, chosen,
           whole_put, half_put, whole_back, half_back, passed, passed_mate, part, part_in, product, want, wants,
           grams, gram_in, gram_sum, gram_near, gram_part, gram_all, ns, roots,
           stage_sem, send_sem, recv_sem, fence_sem):
    wide, narrow, cuts = routes.wide, routes.narrow, routes.cuts
    me_w = lax.axis_index("wide")
    me_z = lax.axis_index("narrow")
    order = tile_hi.shape[0]
    rows, width = start.shape
    n = rows // cuts
    wbits = routes.wbits
    f32 = jnp.float32
    slice_rows = width // wide
    total_rows = float(wide * order)
    whole_at = {unit: place for place, unit in enumerate(routes.whole)}
    half_at = {unit: place for place, unit in enumerate(routes.half)}

    def wide_peer(mask):
        return {"wide": flip(me_w, mask), "narrow": me_z}

    def near_peer(mask):
        return {"wide": me_w, "narrow": flip(me_z, mask)}

    peers = [wide_peer(m) for m in range(1, wide)] + [near_peer(m) for m in range(1, narrow)]
    barrier = pltpu.get_barrier_semaphore()
    for peer in peers:
        pl.semaphore_signal(barrier, inc=1, device_id=peer, device_id_type=MESH)

    stage_rows = stage.shape[1]
    stages = stage.shape[0]

    def fetch(chunk):
        return pltpu.make_async_copy(
            tile_hbm.at[pl.ds(chunk * stage_rows, stage_rows)],
            stage.at[chunk % stages],
            stage_sem.at[chunk % stages],
        )

    for chunk in range(stages):
        fetch(chunk).start()

    mate = flip(me_z, 1)
    own_want = row_columns[0, me_z] ^ me_w
    mate_want = row_columns[0, mate] ^ me_w
    want[...] = jnp.full(want.shape, own_want, jnp.int32)
    pl.semaphore_wait(barrier, len(peers))

    sent = {}
    waited = set()

    def send(name, source, target, peer):
        index = len(sent)
        copy = pltpu.make_async_remote_copy(
            src_ref=source, dst_ref=target, send_sem=send_sem.at[index], recv_sem=recv_sem.at[index],
            device_id=peer, device_id_type=MESH,
        )
        copy.start()
        assert name not in sent
        sent[name] = copy

    def received(name):
        sent[name].wait_recv()

    def all_gone():
        for name, copy in sent.items():
            if name not in waited:
                copy.wait_send()
                waited.add(name)

    for side in range(2):
        send(("want", side), want, wants.at[side], wide_peer(1 << routes.lines[side][-1]))
    wants_here = set()

    def natural(q):
        return pl.multiple_of(flip(me_z, q) * rows, rows)

    def piece_at(q, c):
        return pl.ds(pl.multiple_of(natural(q) + c * n, n), n)

    def here(it):
        return it % slots

    def gathered(it, q, c):
        if routes.paired(q, c):
            return whole_in.at[here(it), whole_at[q, c]]
        return half_in.at[here(it), half_at[q, c]]

    def row_ref(it, q, c):
        if routes.paired(q, c) and q % 2 == 1:
            return mate_rows.at[here(it), whole_at[q - 1, c]]
        return gathered(it, q, c).at[0]

    def put_ref(it, q, c):
        if routes.paired(q, c):
            return whole_put.at[here(it), whole_at[q, c]]
        return half_put.at[here(it), half_at[q, c]]

    def back_ref(it, q, c):
        if routes.paired(q, c):
            return whole_back.at[here(it), whole_at[q, c]]
        return half_back.at[here(it), half_at[q, c]]

    def keep_split(target, at, value):
        hi, lo = split(value)
        target[at, pl.ds(0, width)] = hi
        target[at, pl.ds(width, width)] = lo

    def far_codes(q, c):
        side = routes.side(q, c)
        if side not in wants_here:
            received(("want", side))
            wants_here.add(side)
        code = wants[side, pl.ds(0, 1), :]
        place = position(code, routes.order(q, c))
        place = jnp.where((code >> routes.last(q, c)) & 1 == 1, place, wide)
        return jnp.broadcast_to(place, (n, width))

    def choose(ref, count, place):
        value = ref[0]
        for p in range(1, count):
            value = jnp.where(place == p, ref[p], value)
        return value

    def start_step(it, q, c, level):
        ref = gathered(it, q, c)
        count = 1 << level
        send(
            ("gather", it, q, c, level), ref.at[pl.ds(0, count)], ref.at[pl.ds(count, count)],
            wide_peer(1 << routes.order(q, c)[level]),
        )

    def start_back(it, q, c, level):
        count = 1 << level
        send(
            ("back", it, q, c, level), put_ref(it, q, c).at[pl.ds(count, count)],
            back_ref(it, q, c).at[pl.ds(count, count)], wide_peer(1 << routes.order(q, c)[level]),
        )

    def do_load(chunk):
        fetch(chunk).wait()
        hi, lo = split(stage[chunk % stages])
        at = pl.ds(chunk * stage_rows, stage_rows)
        tile_hi[at, :] = hi
        tile_lo[at, :] = lo
        turn_hi[:, at] = hi.T
        turn_lo[:, at] = lo.T
        if chunk + stages < LOAD_CHUNKS:
            fetch(chunk + stages).start()

    def do_turn(it):
        if slots == ITERS:
            return
        all_gone()
        for peer in peers:
            pl.semaphore_signal(fence_sem, inc=1, device_id=peer, device_id_type=MESH)
        pl.semaphore_wait(fence_sem, len(peers))
        for c in range(cuts):
            row_ref(it, 0, c)[...] = product[pl.ds(c * n, n), :]

    def do_have(it, q, c):
        ref = row_ref(it, q, c)
        if q > 0:
            received(("rows", it, q, c))
        elif it == 0:
            ref[...] = start[pl.ds(c * n, n), :]
        for child in routes.children(q):
            send(("rows", it, child, c), ref, row_ref(it, child, c), near_peer(child ^ q))
        if not (routes.paired(q, c) and q % 2 == 1):
            start_step(it, q, c, 0)
        keep_split(rows_right, piece_at(q, c), ref[...])

    def do_step(it, q, c, level):
        received(("gather", it, q, c, level - 1))
        start_step(it, q, c, level)

    def do_pick(it, q, c):
        levels = len(routes.order(q, c))
        received(("gather", it, q, c, levels - 1))
        if routes.paired(q, c):
            at = whole_at[q, c]
            picks[here(it), at] = choose(gathered(it, q, c), wide, position(mate_want, routes.order(q, c)))
            send(("pick", it, q, c), picks.at[here(it), at], picked.at[here(it), at], near_peer(1))
        else:
            at = half_at[q, c]
            choices[here(it), at] = choose(gathered(it, q, c), wide // 2, far_codes(q, c))
            send(
                ("pick", it, q, c), choices.at[here(it), at], chosen.at[here(it), at],
                wide_peer(1 << routes.last(q, c)),
            )

    def do_column(it, q, c):
        if routes.paired(q, c):
            if q % 2 == 0:
                value = choose(gathered(it, q, c), wide, position(own_want, routes.order(q, c)))
            else:
                received(("pick", it, q - 1, c))
                value = picked[here(it), whole_at[q - 1, c]]
        else:
            received(("pick", it, q, c))
            value = choose(gathered(it, q, c), wide // 2, position(own_want, routes.order(q, c)))
            value = jnp.where((own_want >> routes.last(q, c)) & 1 == 1, chosen[here(it), half_at[q, c]], value)
        keep_split(columns_right, piece_at(q, c), value)

    def product_of(hi, lo, right, at):
        both = jnp.dot(hi[at, :], right[...], preferred_element_type=f32)
        rest = jnp.dot(lo[at, :], right[:, pl.ds(0, width)], preferred_element_type=f32)
        return both[:, :width] + (both[:, width:] + rest)

    def do_trans(it, q):
        at = pl.ds(natural(q), rows)
        trans[here(it), at, :] = product_of(turn_hi, turn_lo, rows_right, at)

    def do_direct(it, q):
        at = pl.ds(natural(q), rows)
        direct[at, :] = product_of(tile_hi, tile_lo, columns_right, at)

    def do_pass(it, q, c):
        source = trans.at[here(it), piece_at(q, c)]
        if routes.paired(q, c):
            send(("pass", it, q, c), source, passed_mate.at[here(it), whole_at[q - 1, c]], near_peer(1))
        else:
            send(
                ("pass", it, q, c), source, passed.at[here(it), half_at[q, c]],
                wide_peer(1 << routes.last(q, c)),
            )

    def do_put(it, q, c):
        mine = trans[here(it), piece_at(q, c), :]
        ref = put_ref(it, q, c)
        places = routes.order(q, c)
        if routes.paired(q, c):
            received(("pass", it, q + 1, c))
            other = passed_mate[here(it), whole_at[q, c]]
            count, first, second = wide, position(own_want, places), position(mate_want, places)
        else:
            received(("pass", it, q, c))
            other = passed[here(it), half_at[q, c]]
            count, second = wide // 2, far_codes(q, c)
            first = position(own_want, places) + wide * ((own_want >> routes.last(q, c)) & 1)
        for p in range(count):
            ref[p] = jnp.where(first == p, mine, 0.0) + jnp.where(second == p, other, 0.0)
        start_back(it, q, c, len(places) - 1)

    def do_down(it, q, c, level):
        received(("back", it, q, c, level))
        count = 1 << level
        ref, came = put_ref(it, q, c), back_ref(it, q, c)
        for p in range(count):
            ref[p] = ref[p] + came[count + p]
        start_back(it, q, c, level - 1)

    def do_merge(it, q, c):
        value = direct[piece_at(q, c), :]
        if not (routes.paired(q, c) and q % 2 == 1):
            received(("back", it, q, c, 0))
            value = value + (put_ref(it, q, c)[0] + back_ref(it, q, c)[1])
        for child in routes.children(q):
            received(("part", it, child, c))
            value = value + part_in[here(it), child - 1, c]
        if q > 0:
            bit = 1 << lowest(q, routes.nbits)
            part[here(it), q - 1, c] = value
            send(("part", it, q, c), part.at[here(it), q - 1, c], part_in.at[here(it), q - 1, c], near_peer(bit))
        elif it < ITERS - 1:
            product[pl.ds(c * n, n), :] = value
            if slots == ITERS:
                row_ref(it + 1, 0, c)[...] = value
        else:
            product[pl.ds(c * n, n), :] = jnp.dot(value, roots[it - 1], precision=HIGHEST)

    grams_begun = set()

    def do_gram(it, c):
        value = product[pl.ds(c * n, n), :]
        square = lax.dot_general(value, value, (((0,), (0,)), ((), ())), precision=HIGHEST, preferred_element_type=f32)
        if it in grams_begun:
            grams[it] = grams[it] + square
        else:
            grams[it] = square
        grams_begun.add(it)

    def slice_of(mask):
        return pl.ds(pl.multiple_of(flip(me_w, mask) * slice_rows, slice_rows), slice_rows)

    def do_spread(it):
        for mask in range(1, wide):
            send(("spread", it, mask), grams.at[it, slice_of(mask)], gram_in.at[it, mask], wide_peer(mask))

    def do_sum(it):
        values = [grams[it, slice_of(0), :]]
        for mask in range(1, wide):
            received(("spread", it, mask))
            values.append(gram_in[it, mask])
        gram_sum[it] = tree_sum(values)
        for mask in range(1, narrow):
            send(("near", it, mask), gram_sum.at[it], gram_near.at[it, mask], near_peer(mask))

    def do_all(it):
        values = [gram_sum[it]]
        for mask in range(1, narrow):
            received(("near", it, mask))
            values.append(gram_near[it, mask])
        gram_part[it] = tree_sum(values)
        for mask in range(1, wide):
            send(("all", it, mask), gram_part.at[it], gram_all.at[it, slice_of(0)], wide_peer(mask))
        gram_all[it, slice_of(0), :] = gram_part[it]

    def identity():
        row = lax.broadcasted_iota(jnp.int32, (width, width), 0)
        column = lax.broadcasted_iota(jnp.int32, (width, width), 1)
        return jnp.where(row == column, 1.0, 0.0).astype(f32)

    def do_root(it, repeat):
        if repeat == 0:
            for mask in range(1, wide):
                received(("all", it, mask))
            gram = gram_all[it]
            square = jnp.sum(gram * gram, axis=1, keepdims=True)
            scale = jnp.sqrt(jnp.sum(square, axis=0, keepdims=True) + 1e-06)
            current = gram / scale
            middle = 1.5 * identity() - 0.5 * current
            inverse = middle
            ns[2] = jnp.broadcast_to(jnp.sqrt(total_rows / scale), (width, width))
        else:
            current, inverse = ns[0], ns[1]
            middle = 1.5 * identity() - 0.5 * jnp.dot(inverse, current, precision=HIGHEST)
            inverse = jnp.dot(middle, inverse, precision=HIGHEST)
        if repeat < NS_STEPS - 1:
            ns[0] = jnp.dot(current, middle, precision=HIGHEST)
            ns[1] = inverse
        else:
            roots[it] = inverse * ns[2]

    actions = dict(
        load=do_load, turn=do_turn, have=do_have, step=do_step, pick=do_pick, column=do_column, trans=do_trans,
        direct=do_direct, put=do_put, down=do_down, merge=do_merge, gram=do_gram, spread=do_spread, sum=do_sum,
        all=do_all, root=do_root,
    )
    actions["pass"] = do_pass
    for name in sequence:
        actions[name[0]](*name[1:])
    out[...] = jnp.dot(product[...], roots[ITERS - 1], precision=HIGHEST)
    all_gone()


def on_device(hamiltonian_tiles, row_columns, start_vectors):
    wide, narrow = lax.axis_size("wide"), lax.axis_size("narrow")
    order = hamiltonian_tiles.shape[0]
    rows, width = start_vectors.shape
    assert rows * narrow == order
    routes = Routes(wide, narrow)
    cuts = routes.cuts
    n = rows // cuts
    slots = ITERS if narrow <= 4 else 1
    sequence = steps_of(routes)
    if len(ORDER) == len(sequence):
        sequence = [sequence[place] for place in ORDER]
    copies = sends_of(routes)
    wholes, halves = max(1, len(routes.whole)), max(1, len(routes.half))
    f32, bf16 = jnp.float32, jnp.bfloat16
    stage_rows = order // LOAD_CHUNKS
    slice_rows = width // wide

    def vmem(*shape, dtype=f32):
        return pltpu.VMEM(shape, dtype)

    return pl.pallas_call(
        functools.partial(kernel, routes, sequence, slots),
        out_shape=jax.ShapeDtypeStruct((rows, width), f32),
        in_specs=[
            pl.BlockSpec(memory_space=pltpu.SMEM),
            pl.BlockSpec(memory_space=pl.ANY),
            pl.BlockSpec(memory_space=pltpu.VMEM),
        ],
        out_specs=pl.BlockSpec(memory_space=pltpu.VMEM),
        scratch_shapes=[
            vmem(2, stage_rows, order),
            vmem(order, order, dtype=bf16),
            vmem(order, order, dtype=bf16),
            vmem(order, order, dtype=bf16),
            vmem(order, order, dtype=bf16),
            vmem(order, 2 * width, dtype=bf16),
            vmem(order, 2 * width, dtype=bf16),
            vmem(slots, order, width),
            vmem(order, width),
            vmem(slots, wholes, wide, n, width),
            vmem(slots, halves, wide // 2, n, width),
            vmem(slots, wholes, n, width),
            vmem(slots, wholes, n, width),
            vmem(slots, wholes, n, width),
            vmem(slots, halves, n, width),
            vmem(slots, halves, n, width),
            vmem(slots, wholes, wide, n, width),
            vmem(slots, halves, wide // 2, n, width),
            vmem(slots, wholes, wide, n, width),
            vmem(slots, halves, wide // 2, n, width),
            vmem(slots, halves, n, width),
            vmem(slots, wholes, n, width),
            vmem(slots, narrow - 1, cuts, n, width),
            vmem(slots, narrow - 1, cuts, n, width),
            vmem(rows, width),
            vmem(8, 128, dtype=jnp.int32),
            vmem(2, 8, 128, dtype=jnp.int32),
            vmem(ITERS, width, width),
            vmem(ITERS, wide, slice_rows, width),
            vmem(ITERS, slice_rows, width),
            vmem(ITERS, narrow, slice_rows, width),
            vmem(ITERS, slice_rows, width),
            vmem(ITERS, width, width),
            vmem(3, width, width),
            vmem(ITERS, width, width),
            pltpu.SemaphoreType.DMA((2,)),
            pltpu.SemaphoreType.DMA((copies,)),
            pltpu.SemaphoreType.DMA((copies,)),
            pltpu.SemaphoreType.REGULAR,
        ],
        compiler_params=pltpu.CompilerParams(
            collective_id=0, has_side_effects=True, vmem_limit_bytes=67043328
        ),
    )(row_columns, hamiltonian_tiles, start_vectors)


def solution(mesh):
    return jax.shard_map(
        on_device,
        mesh=mesh,
        in_specs=(P("wide", "narrow"), P("wide", None), P(("wide", "narrow"), None)),
        out_specs=P(("wide", "narrow"), None),
        check_vma=False,
    )
```

```python
import functools

import jax
import jax.numpy as jnp
from jax import lax
from jax.experimental import pallas as pl
from jax.experimental.pallas import tpu as pltpu
from jax.sharding import PartitionSpec as P

ITERS = 2
SHARES = 2
NS_STEPS = 5
HIGHEST = lax.Precision.HIGHEST
MESH = pl.DeviceIdType.MESH
LOAD_CHUNKS = 6
ORDER = (
    9, 8, 7, 0, 1, 25, 2, 17, 23, 24, 3, 4, 13, 16, 5, 6, 37, 11, 12, 29, 15, 41, 73, 21,
    45, 35, 36, 20, 51, 54, 55, 63, 67, 22, 57, 60, 14, 61, 10, 28, 66, 19, 40, 33, 39, 32, 69, 44,
    72, 97, 140, 96, 49, 77, 105, 48, 113, 18, 62, 68, 50, 64, 76, 65, 112, 53, 81, 101, 80, 109, 84, 85,
    87, 125, 117, 104, 100, 52, 56, 31, 124, 108, 116, 91, 133, 30, 89, 129, 121, 59, 27, 47, 34, 46, 132, 95,
    93, 58, 128, 71, 94, 26, 120, 43, 38, 70, 103, 111, 42, 137, 144, 110, 99, 102, 107, 75, 83, 98, 115, 136,
    143, 82, 79, 74, 78, 86, 123, 114, 106, 160, 122, 152, 92, 151, 88, 127, 119, 90, 131, 148, 147, 159, 126, 118,
    156, 130, 164, 155, 186, 190, 189, 192, 196, 163, 135, 142, 180, 139, 204, 179, 171, 168, 195, 134, 141, 231, 198, 167,
    236, 172, 158, 184, 201, 138, 232, 150, 257, 215, 216, 157, 183, 235, 146, 252, 149, 175, 176, 251, 202, 220, 239, 170,
    247, 207, 248, 145, 208, 162, 154, 258, 174, 206, 219, 153, 203, 185, 161, 211, 188, 187, 197, 199, 191, 200, 212, 169,
    177, 178, 222, 268, 165, 173, 267, 166, 193, 205, 230, 229, 194, 226, 275, 182, 181, 240, 238, 246, 245, 224, 237, 243,
    244, 272, 214, 210, 233, 276, 209, 213, 218, 217, 221, 265, 241, 249, 266, 271, 234, 242, 225, 250, 273, 223, 259, 269,
    255, 256, 274, 228, 227, 253, 270, 254, 260, 261, 280, 262, 263, 264, 277, 279, 281, 278, 282, 283, 284, 285, 286, 287,
    288, 289, 290,
)


def flip(x, mask):
    bit = 1
    while bit <= mask:
        if mask & bit:
            x = x + bit * (1 - 2 * ((x // bit) % 2))
        bit *= 2
    return x


def bits_of(count):
    bits = count.bit_length() - 1
    assert count == 1 << bits
    return bits


def position(relative, order):
    return sum(((relative >> bit) & 1) << place for place, bit in enumerate(order))


class Routes:
    def __init__(self, wide, narrow):
        self.wide, self.narrow = wide, narrow
        self.wbits, self.nbits = bits_of(wide), bits_of(narrow)
        self.cuts = max(SHARES, 4 * 4 // narrow)
        self.run = self.cuts // SHARES
        upper = list(range(1, self.wbits))
        self.lines = [upper, upper[::-1]]
        self.whole = []
        self.half = []
        for q in range(narrow):
            for c in range(self.cuts):
                if self.paired(q, c):
                    if q % 2 == 0:
                        self.whole.append((q, c))
                else:
                    self.half.append((q, c))

    def side(self, q, c):
        return (q + c) % 2

    def share(self, c):
        return c // self.run

    def paired(self, q, c):
        return q < 2

    def order(self, q, c):
        line = self.lines[self.side(q, c)]
        return line + [0] if self.paired(q, c) else line[:-1] + [0]

    def last(self, q, c):
        return self.lines[self.side(q, c)][-1]

    def straight(self, c):
        return False

    def parent(self, q, c):
        return 0 if self.straight(c) else q & (q - 1)

    def children(self, q, c):
        return [other for other in range(self.narrow - 1, 0, -1) if self.parent(other, c) == q]


def steps_of(routes):
    quarters, cuts = range(routes.narrow), range(routes.cuts)
    steps = [("load", i) for i in range(LOAD_CHUNKS)]
    for it in range(ITERS):
        if it > 0:
            steps.append(("turn", it))
        for q in quarters:
            for c in cuts:
                steps.append(("have", it, q, c))
        for level in range(1, routes.wbits):
            for q in quarters:
                for c in cuts:
                    paired = routes.paired(q, c)
                    if paired and q % 2 == 1:
                        continue
                    if level < len(routes.order(q, c)):
                        steps.append(("step", it, q, c, level))
        for q in quarters:
            for c in cuts:
                if not (routes.paired(q, c) and q % 2 == 1):
                    steps.append(("pick", it, q, c))
        for q in quarters[::-1]:
            for share in range(SHARES):
                steps.append(("trans", it, q, share))
            for c in cuts:
                if not (routes.paired(q, c) and q % 2 == 0):
                    steps.append(("pass", it, q, c))
        for q in quarters:
            for c in cuts:
                steps.append(("column", it, q, c))
        for q in quarters[::-1]:
            for share in range(SHARES):
                steps.append(("direct", it, q, share))
        for q in quarters[::-1]:
            for c in cuts:
                if not (routes.paired(q, c) and q % 2 == 1):
                    steps.append(("put", it, q, c))
        for level in range(routes.wbits - 1, 0, -1):
            for q in quarters[::-1]:
                for c in cuts:
                    if routes.paired(q, c) and q % 2 == 1:
                        continue
                    if level < len(routes.order(q, c)):
                        steps.append(("down", it, q, c, level))
        if it > 0:
            steps.append(("spread", it - 1))
            steps.append(("sum", it - 1))
            steps.append(("all", it - 1))
            steps += [("root", it - 1, repeat) for repeat in range(NS_STEPS)]
        for q in quarters[::-1]:
            for c in cuts:
                steps.append(("merge", it, q, c))
        for c in range(routes.run):
            steps.append(("gram", it, c))
    steps.append(("spread", ITERS - 1))
    steps.append(("sum", ITERS - 1))
    steps.append(("all", ITERS - 1))
    steps += [("root", ITERS - 1, repeat) for repeat in range(NS_STEPS)]
    return steps


def sends_of(routes):
    count = 2
    pieces = routes.narrow * routes.cuts
    for it in range(ITERS):
        count += 2 * (routes.narrow - 1) * routes.cuts
        count += 2 * len(routes.whole) * (routes.wbits + 1)
        count += 2 * len(routes.half) * routes.wbits
        count += 2 * (routes.wide - 1) + routes.narrow - 1
    return count


def split(x):
    high = x.astype(jnp.bfloat16)
    low = (x - high.astype(jnp.float32)).astype(jnp.bfloat16)
    return high, low


def tree_sum(values):
    while len(values) > 1:
        values = [a + b for a, b in zip(values[::2], values[1::2])]
    return values[0]


def kernel(routes, sequence, slots, row_columns, tile_hbm, start, out, stage, tile_hi, tile_lo, turn_hi, turn_lo,
           rows_right, columns_right, trans, direct, whole_in, half_in, mate_rows, picks, picked, choices, chosen,
           whole_put, half_put, whole_back, half_back, passed, passed_mate, part, part_in, product, turned, want, wants,
           grams, gram_in, gram_sum, gram_near, gram_part, gram_all, ns, roots,
           stage_sem, send_sem, recv_sem, fence_sem):
    wide, narrow, cuts = routes.wide, routes.narrow, routes.cuts
    me_w = lax.axis_index("wide")
    me_z = lax.axis_index("narrow")
    order = tile_hi.shape[0]
    rows, width = start.shape
    n = rows // cuts
    wbits = routes.wbits
    f32 = jnp.float32
    slice_rows = width // wide
    total_rows = float(wide * order)
    run = routes.run
    half_width = width // SHARES
    first_lanes = lax.broadcasted_iota(jnp.int32, (n, width), 1) < half_width
    whole_at = {unit: place for place, unit in enumerate(routes.whole)}
    half_at = {unit: place for place, unit in enumerate(routes.half)}

    def wide_peer(mask):
        return {"wide": flip(me_w, mask), "narrow": me_z}

    def near_peer(mask):
        return {"wide": me_w, "narrow": flip(me_z, mask)}

    peers = [wide_peer(m) for m in range(1, wide)] + [near_peer(m) for m in range(1, narrow)]
    barrier = pltpu.get_barrier_semaphore()
    for peer in peers:
        pl.semaphore_signal(barrier, inc=1, device_id=peer, device_id_type=MESH)

    stage_rows = stage.shape[1]
    stages = stage.shape[0]

    def fetch(chunk):
        return pltpu.make_async_copy(
            tile_hbm.at[pl.ds(chunk * stage_rows, stage_rows)],
            stage.at[chunk % stages],
            stage_sem.at[chunk % stages],
        )

    for chunk in range(stages):
        fetch(chunk).start()

    mate = flip(me_z, 1)
    own_want = row_columns[0, me_z] ^ me_w
    mate_want = row_columns[0, mate] ^ me_w
    want[...] = jnp.full(want.shape, own_want, jnp.int32)
    pl.semaphore_wait(barrier, len(peers))

    sent = {}
    waited = set()

    def send(name, source, target, peer):
        index = len(sent)
        copy = pltpu.make_async_remote_copy(
            src_ref=source, dst_ref=target, send_sem=send_sem.at[index], recv_sem=recv_sem.at[index],
            device_id=peer, device_id_type=MESH,
        )
        copy.start()
        assert name not in sent
        sent[name] = copy

    def received(name):
        sent[name].wait_recv()

    def all_gone():
        for name, copy in sent.items():
            if name not in waited:
                copy.wait_send()
                waited.add(name)

    for side in range(2):
        send(("want", side), want, wants.at[side], wide_peer(1 << routes.lines[side][-1]))
    wants_here = set()

    def natural(q):
        return pl.multiple_of(flip(me_z, q) * rows, rows)

    def swap(x):
        return pltpu.roll(x, half_width, 1)

    def rows_of(c):
        at = (c % run) * 2 * n
        return at, at + n

    def here(it):
        return it % slots

    def gathered(it, q, c):
        if routes.paired(q, c):
            return whole_in.at[here(it), whole_at[q, c]]
        return half_in.at[here(it), half_at[q, c]]

    def row_ref(it, q, c):
        if routes.paired(q, c) and q % 2 == 1:
            return mate_rows.at[here(it), whole_at[q - 1, c]]
        return gathered(it, q, c).at[0]

    def put_ref(it, q, c):
        if routes.paired(q, c):
            return whole_put.at[here(it), whole_at[q, c]]
        return half_put.at[here(it), half_at[q, c]]

    def back_ref(it, q, c):
        if routes.paired(q, c):
            return whole_back.at[here(it), whole_at[q, c]]
        return half_back.at[here(it), half_at[q, c]]

    def keep_split(target, q, c, value):
        hi = value.astype(jnp.bfloat16).astype(f32)
        lo = value - hi
        first, second = rows_of(c)
        at = pl.ds(pl.multiple_of(natural(q) + first, n), n)
        target[routes.share(c), at, :] = jnp.where(first_lanes, hi, swap(lo)).astype(jnp.bfloat16)
        at = pl.ds(pl.multiple_of(natural(q) + second, n), n)
        target[routes.share(c), at, :] = jnp.where(first_lanes, swap(hi), lo).astype(jnp.bfloat16)

    def far_codes(q, c):
        side = routes.side(q, c)
        if side not in wants_here:
            received(("want", side))
            wants_here.add(side)
        code = wants[side, pl.ds(0, 1), :]
        place = position(code, routes.order(q, c))
        place = jnp.where((code >> routes.last(q, c)) & 1 == 1, place, wide)
        return jnp.broadcast_to(place, (n, width))

    def choose(ref, count, place):
        value = ref[0]
        for p in range(1, count):
            value = jnp.where(place == p, ref[p], value)
        return value

    def start_step(it, q, c, level):
        ref = gathered(it, q, c)
        count = 1 << level
        send(
            ("gather", it, q, c, level), ref.at[pl.ds(0, count)], ref.at[pl.ds(count, count)],
            wide_peer(1 << routes.order(q, c)[level]),
        )

    def start_back(it, q, c, level):
        count = 1 << level
        send(
            ("back", it, q, c, level), put_ref(it, q, c).at[pl.ds(count, count)],
            back_ref(it, q, c).at[pl.ds(count, count)], wide_peer(1 << routes.order(q, c)[level]),
        )

    def do_load(chunk):
        fetch(chunk).wait()
        hi, lo = split(stage[chunk % stages])
        at = pl.ds(chunk * stage_rows, stage_rows)
        tile_hi[at, :] = hi
        tile_lo[at, :] = lo
        turn_hi[:, at] = hi.T
        turn_lo[:, at] = lo.T
        if chunk + stages < LOAD_CHUNKS:
            fetch(chunk + stages).start()

    def do_turn(it):
        if slots == ITERS:
            return
        all_gone()
        for peer in peers:
            pl.semaphore_signal(fence_sem, inc=1, device_id=peer, device_id_type=MESH)
        pl.semaphore_wait(fence_sem, len(peers))
        for c in range(cuts):
            row_ref(it, 0, c)[...] = product[c]

    def do_have(it, q, c):
        ref = row_ref(it, q, c)
        if q > 0:
            received(("rows", it, q, c))
        elif it == 0:
            first, second = (start[pl.ds(at, n), :] for at in rows_of(c))
            if routes.share(c) == 0:
                ref[...] = jnp.where(first_lanes, first, swap(second))
            else:
                ref[...] = jnp.where(first_lanes, swap(first), second)
        for child in routes.children(q, c):
            send(("rows", it, child, c), ref, row_ref(it, child, c), near_peer(child ^ q))
        if not (routes.paired(q, c) and q % 2 == 1):
            start_step(it, q, c, 0)
        keep_split(rows_right, q, c, ref[...])

    def do_step(it, q, c, level):
        received(("gather", it, q, c, level - 1))
        start_step(it, q, c, level)

    def do_pick(it, q, c):
        levels = len(routes.order(q, c))
        received(("gather", it, q, c, levels - 1))
        if routes.paired(q, c):
            at = whole_at[q, c]
            picks[here(it), at] = choose(gathered(it, q, c), wide, position(mate_want, routes.order(q, c)))
            send(("pick", it, q, c), picks.at[here(it), at], picked.at[here(it), at], near_peer(1))
        else:
            at = half_at[q, c]
            choices[here(it), at] = choose(gathered(it, q, c), wide // 2, far_codes(q, c))
            send(
                ("pick", it, q, c), choices.at[here(it), at], chosen.at[here(it), at],
                wide_peer(1 << routes.last(q, c)),
            )

    def do_column(it, q, c):
        if routes.paired(q, c):
            if q % 2 == 0:
                value = choose(gathered(it, q, c), wide, position(own_want, routes.order(q, c)))
            else:
                received(("pick", it, q - 1, c))
                value = picked[here(it), whole_at[q - 1, c]]
        else:
            received(("pick", it, q, c))
            value = choose(gathered(it, q, c), wide // 2, position(own_want, routes.order(q, c)))
            value = jnp.where((own_want >> routes.last(q, c)) & 1 == 1, chosen[here(it), half_at[q, c]], value)
        keep_split(columns_right, q, c, value)

    def product_of(target, q, share, hi, lo, right):
        at = pl.ds(natural(q), rows)
        value = jnp.dot(hi[at, :], right[share], preferred_element_type=f32)
        value = value + jnp.dot(lo[at, :], right[share], preferred_element_type=f32)
        value = value + swap(value)
        for c in range(share * run, (share + 1) * run):
            first, second = rows_of(c)
            target[q, c] = jnp.where(first_lanes, value[first:first + n], value[second:second + n])

    def do_trans(it, q, share):
        product_of(trans.at[here(it)], q, share, turn_hi, turn_lo, rows_right)

    def do_direct(it, q, share):
        product_of(direct, q, share, tile_hi, tile_lo, columns_right)

    def do_pass(it, q, c):
        source = trans.at[here(it), q, c]
        if routes.paired(q, c):
            send(("pass", it, q, c), source, passed_mate.at[here(it), whole_at[q - 1, c]], near_peer(1))
        else:
            send(
                ("pass", it, q, c), source, passed.at[here(it), half_at[q, c]],
                wide_peer(1 << routes.last(q, c)),
            )

    def do_put(it, q, c):
        mine = trans[here(it), q, c]
        ref = put_ref(it, q, c)
        places = routes.order(q, c)
        if routes.paired(q, c):
            received(("pass", it, q + 1, c))
            other = passed_mate[here(it), whole_at[q, c]]
            count, first, second = wide, position(own_want, places), position(mate_want, places)
        else:
            received(("pass", it, q, c))
            other = passed[here(it), half_at[q, c]]
            count, second = wide // 2, far_codes(q, c)
            first = position(own_want, places) + wide * ((own_want >> routes.last(q, c)) & 1)
        for p in range(count):
            ref[p] = jnp.where(first == p, mine, 0.0) + jnp.where(second == p, other, 0.0)
        start_back(it, q, c, len(places) - 1)

    def do_down(it, q, c, level):
        received(("back", it, q, c, level))
        count = 1 << level
        ref, came = put_ref(it, q, c), back_ref(it, q, c)
        for p in range(count):
            ref[p] = ref[p] + came[count + p]
        start_back(it, q, c, level - 1)

    def do_merge(it, q, c):
        value = direct[q, c]
        if not (routes.paired(q, c) and q % 2 == 1):
            received(("back", it, q, c, 0))
            value = value + (put_ref(it, q, c)[0] + back_ref(it, q, c)[1])
        for child in routes.children(q, c):
            received(("part", it, child, c))
            value = value + part_in[here(it), child - 1, c]
        if q > 0:
            part[here(it), q - 1, c] = value
            send(("part", it, q, c), part.at[here(it), q - 1, c], part_in.at[here(it), q - 1, c],
                 near_peer(q ^ routes.parent(q, c)))
        else:
            product[c] = value
            if it < ITERS - 1 and slots == ITERS:
                row_ref(it + 1, 0, c)[...] = value

    grams_begun = set()

    def do_gram(it, c):
        left, right = product[c], product[run + c]
        value = jnp.concatenate(
            [jnp.where(first_lanes, left, swap(right)), jnp.where(first_lanes, swap(left), right)], axis=0
        )
        if it > 0:
            value = jnp.dot(value, roots[it - 1], precision=HIGHEST)
            turned[pl.ds(c * 2 * n, 2 * n), :] = value
        square = lax.dot_general(value, value, (((0,), (0,)), ((), ())), precision=HIGHEST, preferred_element_type=f32)
        if it in grams_begun:
            grams[it] = grams[it] + square
        else:
            grams[it] = square
        grams_begun.add(it)

    def slice_of(mask):
        return pl.ds(pl.multiple_of(flip(me_w, mask) * slice_rows, slice_rows), slice_rows)

    def do_spread(it):
        for mask in range(1, wide):
            send(("spread", it, mask), grams.at[it, slice_of(mask)], gram_in.at[it, mask], wide_peer(mask))

    def do_sum(it):
        values = [grams[it, slice_of(0), :]]
        for mask in range(1, wide):
            received(("spread", it, mask))
            values.append(gram_in[it, mask])
        gram_sum[it] = tree_sum(values)
        for mask in range(1, narrow):
            send(("near", it, mask), gram_sum.at[it], gram_near.at[it, mask], near_peer(mask))

    def do_all(it):
        values = [gram_sum[it]]
        for mask in range(1, narrow):
            received(("near", it, mask))
            values.append(gram_near[it, mask])
        gram_part[it] = tree_sum(values)
        for mask in range(1, wide):
            send(("all", it, mask), gram_part.at[it], gram_all.at[it, slice_of(0)], wide_peer(mask))
        gram_all[it, slice_of(0), :] = gram_part[it]

    def identity():
        row = lax.broadcasted_iota(jnp.int32, (width, width), 0)
        column = lax.broadcasted_iota(jnp.int32, (width, width), 1)
        return jnp.where(row == column, 1.0, 0.0).astype(f32)

    def do_root(it, repeat):
        if repeat == 0:
            for mask in range(1, wide):
                received(("all", it, mask))
            gram = gram_all[it]
            square = jnp.sum(gram * gram, axis=1, keepdims=True)
            scale = jnp.sqrt(jnp.sum(square, axis=0, keepdims=True) + 1e-06)
            current = gram / scale
            middle = 1.5 * identity() - 0.5 * current
            inverse = middle
            ns[2] = jnp.broadcast_to(jnp.sqrt(total_rows / scale), (width, width))
        else:
            current, inverse = ns[0], ns[1]
            middle = 1.5 * identity() - 0.5 * jnp.dot(inverse, current, precision=HIGHEST)
            inverse = jnp.dot(middle, inverse, precision=HIGHEST)
        if repeat < NS_STEPS - 1:
            ns[0] = jnp.dot(current, middle, precision=HIGHEST)
            ns[1] = inverse
        else:
            roots[it] = inverse * ns[2]

    actions = dict(
        load=do_load, turn=do_turn, have=do_have, step=do_step, pick=do_pick, column=do_column, trans=do_trans,
        direct=do_direct, put=do_put, down=do_down, merge=do_merge, gram=do_gram, spread=do_spread, sum=do_sum,
        all=do_all, root=do_root,
    )
    actions["pass"] = do_pass
    for name in sequence:
        actions[name[0]](*name[1:])
    out[...] = jnp.dot(turned[...], roots[ITERS - 1], precision=HIGHEST)
    all_gone()


def on_device(hamiltonian_tiles, row_columns, start_vectors):
    wide, narrow = lax.axis_size("wide"), lax.axis_size("narrow")
    order = hamiltonian_tiles.shape[0]
    rows, width = start_vectors.shape
    assert rows * narrow == order
    routes = Routes(wide, narrow)
    cuts = routes.cuts
    n = rows // cuts
    slots = ITERS if narrow <= 4 else 1
    sequence = steps_of(routes)
    if len(ORDER) == len(sequence):
        sequence = [sequence[place] for place in ORDER]
    copies = sends_of(routes)
    wholes, halves = max(1, len(routes.whole)), max(1, len(routes.half))
    f32, bf16 = jnp.float32, jnp.bfloat16
    stage_rows = order // LOAD_CHUNKS
    slice_rows = width // wide

    def vmem(*shape, dtype=f32):
        return pltpu.VMEM(shape, dtype)

    return pl.pallas_call(
        functools.partial(kernel, routes, sequence, slots),
        out_shape=jax.ShapeDtypeStruct((rows, width), f32),
        in_specs=[
            pl.BlockSpec(memory_space=pltpu.SMEM),
            pl.BlockSpec(memory_space=pl.ANY),
            pl.BlockSpec(memory_space=pltpu.VMEM),
        ],
        out_specs=pl.BlockSpec(memory_space=pltpu.VMEM),
        scratch_shapes=[
            vmem(2, stage_rows, order),
            vmem(order, order, dtype=bf16),
            vmem(order, order, dtype=bf16),
            vmem(order, order, dtype=bf16),
            vmem(order, order, dtype=bf16),
            vmem(SHARES, order, width, dtype=bf16),
            vmem(SHARES, order, width, dtype=bf16),
            vmem(slots, narrow, cuts, n, width),
            vmem(narrow, cuts, n, width),
            vmem(slots, wholes, wide, n, width),
            vmem(slots, halves, wide // 2, n, width),
            vmem(slots, wholes, n, width),
            vmem(slots, wholes, n, width),
            vmem(slots, wholes, n, width),
            vmem(slots, halves, n, width),
            vmem(slots, halves, n, width),
            vmem(slots, wholes, wide, n, width),
            vmem(slots, halves, wide // 2, n, width),
            vmem(slots, wholes, wide, n, width),
            vmem(slots, halves, wide // 2, n, width),
            vmem(slots, halves, n, width),
            vmem(slots, wholes, n, width),
            vmem(slots, narrow - 1, cuts, n, width),
            vmem(slots, narrow - 1, cuts, n, width),
            vmem(cuts, n, width),
            vmem(rows, width),
            vmem(8, 128, dtype=jnp.int32),
            vmem(2, 8, 128, dtype=jnp.int32),
            vmem(ITERS, width, width),
            vmem(ITERS, wide, slice_rows, width),
            vmem(ITERS, slice_rows, width),
            vmem(ITERS, narrow, slice_rows, width),
            vmem(ITERS, slice_rows, width),
            vmem(ITERS, width, width),
            vmem(3, width, width),
            vmem(ITERS, width, width),
            pltpu.SemaphoreType.DMA((2,)),
            pltpu.SemaphoreType.DMA((copies,)),
            pltpu.SemaphoreType.DMA((copies,)),
            pltpu.SemaphoreType.REGULAR,
        ],
        compiler_params=pltpu.CompilerParams(
            collective_id=0, has_side_effects=True, vmem_limit_bytes=67043328
        ),
    )(row_columns, hamiltonian_tiles, start_vectors)


def solution(mesh):
    return jax.shard_map(
        on_device,
        mesh=mesh,
        in_specs=(P("wide", "narrow"), P("wide", None), P(("wide", "narrow"), None)),
        out_specs=P(("wide", "narrow"), None),
        check_vma=False,
    )
```

```python
import functools

import jax
import jax.numpy as jnp
from jax import lax
from jax.experimental import pallas as pl
from jax.experimental.pallas import tpu as pltpu
from jax.sharding import PartitionSpec as P

ITERS = 2
SHARES = 2
NS_STEPS = 5
HIGHEST = lax.Precision.HIGHEST
MESH = pl.DeviceIdType.MESH
LOAD_CHUNKS = 12
ORDER = (
    146, 15, 0, 1, 12, 2, 14, 3, 4, 5, 6, 23, 31, 13, 7, 8, 30, 22, 20, 9, 35, 28, 27, 29,
    16, 43, 18, 10, 11, 21, 42, 19, 26, 57, 61, 60, 69, 72, 63, 66, 46, 39, 24, 34, 25, 17, 62, 47,
    73, 38, 67, 50, 51, 41, 55, 75, 102, 110, 68, 70, 54, 56, 118, 103, 58, 36, 32, 40, 114, 33, 71, 78,
    106, 37, 119, 45, 74, 52, 107, 44, 76, 53, 122, 86, 83, 82, 59, 91, 65, 79, 87, 90, 93, 130, 111, 131,
    49, 123, 97, 139, 109, 48, 126, 115, 100, 138, 108, 89, 95, 77, 116, 134, 80, 64, 112, 135, 88, 85, 81, 101,
    84, 96, 136, 105, 137, 92, 117, 128, 127, 104, 99, 142, 149, 120, 94, 98, 121, 113, 129, 143, 150, 132, 124, 165,
    157, 166, 125, 133, 158, 169, 140, 147, 144, 185, 177, 161, 153, 141, 148, 154, 162, 192, 196, 195, 198, 170, 202, 201,
    163, 155, 178, 204, 207, 173, 186, 156, 152, 189, 145, 182, 174, 263, 181, 213, 159, 242, 238, 190, 164, 167, 210, 151,
    245, 214, 241, 208, 237, 175, 160, 203, 205, 183, 191, 194, 193, 179, 221, 254, 264, 253, 168, 171, 197, 199, 176, 258,
    184, 187, 200, 225, 257, 206, 172, 209, 243, 218, 180, 226, 235, 217, 188, 219, 222, 228, 273, 274, 251, 236, 215, 232,
    239, 265, 249, 244, 252, 220, 282, 230, 281, 223, 255, 216, 212, 224, 211, 227, 271, 277, 246, 248, 247, 240, 229, 256,
    272, 278, 250, 261, 266, 267, 268, 275, 231, 260, 279, 276, 259, 262, 280, 269, 270, 234, 285, 233, 283, 287, 286, 284,
    288, 289, 290, 291, 292, 293, 294, 295, 296,
)


def flip(x, mask):
    bit = 1
    while bit <= mask:
        if mask & bit:
            x = x + bit * (1 - 2 * ((x // bit) % 2))
        bit *= 2
    return x


def bits_of(count):
    bits = count.bit_length() - 1
    assert count == 1 << bits
    return bits


def position(relative, order):
    return sum(((relative >> bit) & 1) << place for place, bit in enumerate(order))


class Routes:
    def __init__(self, wide, narrow):
        self.wide, self.narrow = wide, narrow
        self.wbits, self.nbits = bits_of(wide), bits_of(narrow)
        self.cuts = max(SHARES, 4 * 4 // narrow)
        self.run = self.cuts // SHARES
        upper = list(range(1, self.wbits))
        self.lines = [upper, upper[::-1]]
        self.whole = []
        self.half = []
        for q in range(narrow):
            for c in range(self.cuts):
                if self.paired(q, c):
                    if q % 2 == 0:
                        self.whole.append((q, c))
                else:
                    self.half.append((q, c))

    def side(self, q, c):
        return (q + c) % 2

    def share(self, c):
        return c // self.run

    def paired(self, q, c):
        return q < 2

    def order(self, q, c):
        line = self.lines[self.side(q, c)]
        return line + [0] if self.paired(q, c) else line[:-1] + [0]

    def last(self, q, c):
        return self.lines[self.side(q, c)][-1]

    def straight(self, c):
        return False

    def parent(self, q, c):
        return 0 if self.straight(c) else q & (q - 1)

    def children(self, q, c):
        return [other for other in range(self.narrow - 1, 0, -1) if self.parent(other, c) == q]


def steps_of(routes):
    quarters, cuts = range(routes.narrow), range(routes.cuts)
    steps = [("load", i) for i in range(LOAD_CHUNKS)]
    for it in range(ITERS):
        if it > 0:
            steps.append(("turn", it))
        for q in quarters:
            for c in cuts:
                steps.append(("have", it, q, c))
        for level in range(1, routes.wbits):
            for q in quarters:
                for c in cuts:
                    paired = routes.paired(q, c)
                    if paired and q % 2 == 1:
                        continue
                    if level < len(routes.order(q, c)):
                        steps.append(("step", it, q, c, level))
        for q in quarters:
            for c in cuts:
                if not (routes.paired(q, c) and q % 2 == 1):
                    steps.append(("pick", it, q, c))
        for q in quarters[::-1]:
            for share in range(SHARES):
                steps.append(("trans", it, q, share))
            for c in cuts:
                if not (routes.paired(q, c) and q % 2 == 0):
                    steps.append(("pass", it, q, c))
        for q in quarters:
            for c in cuts:
                steps.append(("column", it, q, c))
        for q in quarters[::-1]:
            for share in range(SHARES):
                steps.append(("direct", it, q, share))
        for q in quarters[::-1]:
            for c in cuts:
                if not (routes.paired(q, c) and q % 2 == 1):
                    steps.append(("put", it, q, c))
        for level in range(routes.wbits - 1, 0, -1):
            for q in quarters[::-1]:
                for c in cuts:
                    if routes.paired(q, c) and q % 2 == 1:
                        continue
                    if level < len(routes.order(q, c)):
                        steps.append(("down", it, q, c, level))
        if it > 0:
            steps.append(("spread", it - 1))
            steps.append(("sum", it - 1))
            steps.append(("all", it - 1))
            steps += [("root", it - 1, repeat) for repeat in range(NS_STEPS)]
        for q in quarters[::-1]:
            for c in cuts:
                steps.append(("merge", it, q, c))
        for c in range(routes.run):
            steps.append(("gram", it, c))
    steps.append(("spread", ITERS - 1))
    steps.append(("sum", ITERS - 1))
    steps.append(("all", ITERS - 1))
    steps += [("root", ITERS - 1, repeat) for repeat in range(NS_STEPS)]
    return steps


def sends_of(routes):
    count = 2
    pieces = routes.narrow * routes.cuts
    for it in range(ITERS):
        count += 2 * (routes.narrow - 1) * routes.cuts
        count += 2 * len(routes.whole) * (routes.wbits + 1)
        count += 2 * len(routes.half) * routes.wbits
        count += 2 * (routes.wide - 1) + routes.narrow - 1
    return count


def split(x):
    high = x.astype(jnp.bfloat16)
    low = (x - high.astype(jnp.float32)).astype(jnp.bfloat16)
    return high, low


def split_dot(a, b):
    a_high, a_low = split(a)
    b_high, b_low = split(b)
    left = jnp.concatenate([a_high, a_low], axis=1)
    right = jnp.concatenate(
        [jnp.concatenate([b_high, b_low], axis=1), jnp.concatenate([b_high, jnp.zeros_like(b_low)], axis=1)], axis=0
    )
    both = jnp.dot(left, right, preferred_element_type=jnp.float32)
    return both[:, : b.shape[1]] + both[:, b.shape[1]:]


def tree_sum(values):
    while len(values) > 1:
        values = [a + b for a, b in zip(values[::2], values[1::2])]
    return values[0]


def kernel(routes, sequence, slots, row_columns, tile_hbm, start_hbm, out, start, stage, tile_hi, tile_lo, turn_hi, turn_lo,
           rows_right, columns_right, trans, direct, whole_in, half_in, mate_rows, picks, picked, choices, chosen,
           whole_put, half_put, whole_back, half_back, passed, passed_mate, part, part_in, product, turned, want, wants,
           grams, gram_in, gram_sum, gram_near, gram_part, gram_all, ns, roots,
           stage_sem, start_sem, send_sem, recv_sem, fence_sem):
    wide, narrow, cuts = routes.wide, routes.narrow, routes.cuts
    me_w = lax.axis_index("wide")
    me_z = lax.axis_index("narrow")
    order = tile_hi.shape[0]
    rows, width = start.shape
    n = rows // cuts
    wbits = routes.wbits
    f32 = jnp.float32
    slice_rows = width // wide
    total_rows = float(wide * order)
    run = routes.run
    half_width = width // SHARES
    first_lanes = lax.broadcasted_iota(jnp.int32, (n, width), 1) < half_width
    whole_at = {unit: place for place, unit in enumerate(routes.whole)}
    half_at = {unit: place for place, unit in enumerate(routes.half)}

    def wide_peer(mask):
        return {"wide": flip(me_w, mask), "narrow": me_z}

    def near_peer(mask):
        return {"wide": me_w, "narrow": flip(me_z, mask)}

    peers = [wide_peer(m) for m in range(1, wide)] + [near_peer(m) for m in range(1, narrow)]
    barrier = pltpu.get_barrier_semaphore()
    for peer in peers:
        pl.semaphore_signal(barrier, inc=1, device_id=peer, device_id_type=MESH)

    stage_rows = stage.shape[1]
    stages = stage.shape[0]

    def fetch(chunk):
        return pltpu.make_async_copy(
            tile_hbm.at[pl.ds(chunk * stage_rows, stage_rows)],
            stage.at[chunk % stages],
            stage_sem.at[chunk % stages],
        )

    begin = pltpu.make_async_copy(start_hbm, start, start_sem)
    begin.start()
    for chunk in range(stages):
        fetch(chunk).start()

    mate = flip(me_z, 1)
    own_want = row_columns[0, me_z] ^ me_w
    mate_want = row_columns[0, mate] ^ me_w
    want[...] = jnp.full(want.shape, own_want, jnp.int32)
    pl.semaphore_wait(barrier, len(peers))

    sent = {}
    waited = set()

    def send(name, source, target, peer):
        index = len(sent)
        copy = pltpu.make_async_remote_copy(
            src_ref=source, dst_ref=target, send_sem=send_sem.at[index], recv_sem=recv_sem.at[index],
            device_id=peer, device_id_type=MESH,
        )
        copy.start()
        assert name not in sent
        sent[name] = copy

    def received(name):
        sent[name].wait_recv()

    def all_gone(*spared):
        for name, copy in sent.items():
            if name not in waited and name[0] not in spared:
                copy.wait_send()
                waited.add(name)

    begin.wait()
    for side in range(2):
        send(("want", side), want, wants.at[side], wide_peer(1 << routes.lines[side][-1]))
    wants_here = set()

    def natural(q):
        return pl.multiple_of(flip(me_z, q) * rows, rows)

    def swap(x):
        return pltpu.roll(x, half_width, 1)

    def rows_of(c):
        at = (c % run) * 2 * n
        return at, at + n

    def here(it):
        return it % slots

    def gathered(it, q, c):
        if routes.paired(q, c):
            return whole_in.at[here(it), whole_at[q, c]]
        return half_in.at[here(it), half_at[q, c]]

    def row_ref(it, q, c):
        if routes.paired(q, c) and q % 2 == 1:
            return mate_rows.at[here(it), whole_at[q - 1, c]]
        return gathered(it, q, c).at[0]

    def put_ref(it, q, c):
        if routes.paired(q, c):
            return whole_put.at[here(it), whole_at[q, c]]
        return half_put.at[here(it), half_at[q, c]]

    def back_ref(it, q, c):
        if routes.paired(q, c):
            return whole_back.at[here(it), whole_at[q, c]]
        return half_back.at[here(it), half_at[q, c]]

    def keep_split(target, q, c, value):
        hi = value.astype(jnp.bfloat16).astype(f32)
        lo = value - hi
        first, second = rows_of(c)
        at = pl.ds(pl.multiple_of(natural(q) + first, n), n)
        target[routes.share(c), at, :] = jnp.where(first_lanes, hi, swap(lo)).astype(jnp.bfloat16)
        at = pl.ds(pl.multiple_of(natural(q) + second, n), n)
        target[routes.share(c), at, :] = jnp.where(first_lanes, swap(hi), lo).astype(jnp.bfloat16)

    def far_codes(q, c):
        side = routes.side(q, c)
        if side not in wants_here:
            received(("want", side))
            wants_here.add(side)
        code = wants[side, pl.ds(0, 1), :]
        place = position(code, routes.order(q, c))
        place = jnp.where((code >> routes.last(q, c)) & 1 == 1, place, wide)
        return jnp.broadcast_to(place, (n, width))

    def choose(ref, count, place):
        value = ref[0]
        for p in range(1, count):
            value = jnp.where(place == p, ref[p], value)
        return value

    def start_step(it, q, c, level):
        ref = gathered(it, q, c)
        count = 1 << level
        send(
            ("gather", it, q, c, level), ref.at[pl.ds(0, count)], ref.at[pl.ds(count, count)],
            wide_peer(1 << routes.order(q, c)[level]),
        )

    def start_back(it, q, c, level):
        count = 1 << level
        send(
            ("back", it, q, c, level), put_ref(it, q, c).at[pl.ds(count, count)],
            back_ref(it, q, c).at[pl.ds(count, count)], wide_peer(1 << routes.order(q, c)[level]),
        )

    def do_load(chunk):
        fetch(chunk).wait()
        hi, lo = split(stage[chunk % stages])
        at = pl.ds(chunk * stage_rows, stage_rows)
        tile_hi[at, :] = hi
        tile_lo[at, :] = lo
        turn_hi[:, at] = hi.T
        turn_lo[:, at] = lo.T
        if chunk + stages < LOAD_CHUNKS:
            fetch(chunk + stages).start()

    def do_turn(it):
        if slots == ITERS:
            return
        all_gone()
        for peer in peers:
            pl.semaphore_signal(fence_sem, inc=1, device_id=peer, device_id_type=MESH)
        pl.semaphore_wait(fence_sem, len(peers))
        for c in range(cuts):
            row_ref(it, 0, c)[...] = product[c]

    def do_have(it, q, c):
        ref = row_ref(it, q, c)
        if q > 0:
            received(("rows", it, q, c))
        elif it == 0:
            first, second = (start[pl.ds(at, n), :] for at in rows_of(c))
            if routes.share(c) == 0:
                ref[...] = jnp.where(first_lanes, first, swap(second))
            else:
                ref[...] = jnp.where(first_lanes, swap(first), second)
        for child in routes.children(q, c):
            send(("rows", it, child, c), ref, row_ref(it, child, c), near_peer(child ^ q))
        if not (routes.paired(q, c) and q % 2 == 1):
            start_step(it, q, c, 0)
        keep_split(rows_right, q, c, ref[...])

    def do_step(it, q, c, level):
        received(("gather", it, q, c, level - 1))
        start_step(it, q, c, level)

    def do_pick(it, q, c):
        levels = len(routes.order(q, c))
        received(("gather", it, q, c, levels - 1))
        if routes.paired(q, c):
            at = whole_at[q, c]
            picks[here(it), at] = choose(gathered(it, q, c), wide, position(mate_want, routes.order(q, c)))
            send(("pick", it, q, c), picks.at[here(it), at], picked.at[here(it), at], near_peer(1))
        else:
            at = half_at[q, c]
            choices[here(it), at] = choose(gathered(it, q, c), wide // 2, far_codes(q, c))
            send(
                ("pick", it, q, c), choices.at[here(it), at], chosen.at[here(it), at],
                wide_peer(1 << routes.last(q, c)),
            )

    def do_column(it, q, c):
        if routes.paired(q, c):
            if q % 2 == 0:
                value = choose(gathered(it, q, c), wide, position(own_want, routes.order(q, c)))
            else:
                received(("pick", it, q - 1, c))
                value = picked[here(it), whole_at[q - 1, c]]
        else:
            received(("pick", it, q, c))
            value = choose(gathered(it, q, c), wide // 2, position(own_want, routes.order(q, c)))
            value = jnp.where((own_want >> routes.last(q, c)) & 1 == 1, chosen[here(it), half_at[q, c]], value)
        keep_split(columns_right, q, c, value)

    def product_of(target, q, share, hi, lo, right):
        at = pl.ds(natural(q), rows)
        value = jnp.dot(hi[at, :], right[share], preferred_element_type=f32)
        value = value + jnp.dot(lo[at, :], right[share], preferred_element_type=f32)
        value = value + swap(value)
        for c in range(share * run, (share + 1) * run):
            first, second = rows_of(c)
            target[q, c] = jnp.where(first_lanes, value[first:first + n], value[second:second + n])

    def do_trans(it, q, share):
        product_of(trans.at[here(it)], q, share, turn_hi, turn_lo, rows_right)

    def do_direct(it, q, share):
        product_of(direct, q, share, tile_hi, tile_lo, columns_right)

    def do_pass(it, q, c):
        source = trans.at[here(it), q, c]
        if routes.paired(q, c):
            send(("pass", it, q, c), source, passed_mate.at[here(it), whole_at[q - 1, c]], near_peer(1))
        else:
            send(
                ("pass", it, q, c), source, passed.at[here(it), half_at[q, c]],
                wide_peer(1 << routes.last(q, c)),
            )

    def do_put(it, q, c):
        mine = trans[here(it), q, c]
        ref = put_ref(it, q, c)
        places = routes.order(q, c)
        if routes.paired(q, c):
            received(("pass", it, q + 1, c))
            other = passed_mate[here(it), whole_at[q, c]]
            count, first, second = wide, position(own_want, places), position(mate_want, places)
        else:
            received(("pass", it, q, c))
            other = passed[here(it), half_at[q, c]]
            count, second = wide // 2, far_codes(q, c)
            first = position(own_want, places) + wide * ((own_want >> routes.last(q, c)) & 1)
        for p in range(count):
            ref[p] = jnp.where(first == p, mine, 0.0) + jnp.where(second == p, other, 0.0)
        start_back(it, q, c, len(places) - 1)

    def do_down(it, q, c, level):
        received(("back", it, q, c, level))
        count = 1 << level
        ref, came = put_ref(it, q, c), back_ref(it, q, c)
        for p in range(count):
            ref[p] = ref[p] + came[count + p]
        start_back(it, q, c, level - 1)

    def do_merge(it, q, c):
        value = direct[q, c]
        if not (routes.paired(q, c) and q % 2 == 1):
            received(("back", it, q, c, 0))
            value = value + (put_ref(it, q, c)[0] + back_ref(it, q, c)[1])
        for child in routes.children(q, c):
            received(("part", it, child, c))
            value = value + part_in[here(it), child - 1, c]
        if q > 0:
            part[here(it), q - 1, c] = value
            send(("part", it, q, c), part.at[here(it), q - 1, c], part_in.at[here(it), q - 1, c],
                 near_peer(q ^ routes.parent(q, c)))
        else:
            product[c] = value
            if it < ITERS - 1 and slots == ITERS:
                row_ref(it + 1, 0, c)[...] = value

    grams_begun = set()

    def do_gram(it, c):
        left, right = product[c], product[run + c]
        value = jnp.concatenate(
            [jnp.where(first_lanes, left, swap(right)), jnp.where(first_lanes, swap(left), right)], axis=0
        )
        if it > 0:
            value = split_dot(value, roots[it - 1])
            turned[pl.ds(c * 2 * n, 2 * n), :] = value
        square = lax.dot_general(value, value, (((0,), (0,)), ((), ())), precision=HIGHEST, preferred_element_type=f32)
        if it in grams_begun:
            grams[it] = grams[it] + square
        else:
            grams[it] = square
        grams_begun.add(it)

    def slice_of(mask):
        return pl.ds(pl.multiple_of(flip(me_w, mask) * slice_rows, slice_rows), slice_rows)

    def do_spread(it):
        for mask in range(1, wide):
            send(("spread", it, mask), grams.at[it, slice_of(mask)], gram_in.at[it, mask], wide_peer(mask))

    def do_sum(it):
        if it == ITERS - 1:
            all_gone("spread")
        values = [grams[it, slice_of(0), :]]
        for mask in range(1, wide):
            received(("spread", it, mask))
            values.append(gram_in[it, mask])
        gram_sum[it] = tree_sum(values)
        for mask in range(1, narrow):
            send(("near", it, mask), gram_sum.at[it], gram_near.at[it, mask], near_peer(mask))

    def do_all(it):
        if it == ITERS - 1:
            all_gone("near")
        values = [gram_sum[it]]
        for mask in range(1, narrow):
            received(("near", it, mask))
            values.append(gram_near[it, mask])
        gram_part[it] = tree_sum(values)
        for mask in range(1, wide):
            send(("all", it, mask), gram_part.at[it], gram_all.at[it, slice_of(0)], wide_peer(mask))
        gram_all[it, slice_of(0), :] = gram_part[it]

    def identity():
        row = lax.broadcasted_iota(jnp.int32, (width, width), 0)
        column = lax.broadcasted_iota(jnp.int32, (width, width), 1)
        return jnp.where(row == column, 1.0, 0.0).astype(f32)

    def do_root(it, repeat):
        if repeat == 0:
            if it == ITERS - 1:
                all_gone("all")
            for mask in range(1, wide):
                received(("all", it, mask))
            gram = gram_all[it]
            square = jnp.sum(gram * gram, axis=1, keepdims=True)
            scale = jnp.sqrt(jnp.sum(square, axis=0, keepdims=True) + 1e-06)
            current = gram / scale
            middle = 1.5 * identity() - 0.5 * current
            inverse = middle
            ns[2] = jnp.broadcast_to(jnp.sqrt(total_rows / scale), (width, width))
        else:
            current, inverse = ns[0], ns[1]
            middle = 1.5 * identity() - 0.5 * split_dot(inverse, current)
            inverse = split_dot(middle, inverse)
        if repeat < NS_STEPS - 1:
            ns[0] = split_dot(current, middle)
            ns[1] = inverse
        else:
            roots[it] = inverse * ns[2]

    actions = dict(
        load=do_load, turn=do_turn, have=do_have, step=do_step, pick=do_pick, column=do_column, trans=do_trans,
        direct=do_direct, put=do_put, down=do_down, merge=do_merge, gram=do_gram, spread=do_spread, sum=do_sum,
        all=do_all, root=do_root,
    )
    actions["pass"] = do_pass
    for name in sequence:
        actions[name[0]](*name[1:])
    all_gone()
    out[...] = split_dot(turned[...], roots[ITERS - 1])


def on_device(hamiltonian_tiles, row_columns, start_vectors):
    wide, narrow = lax.axis_size("wide"), lax.axis_size("narrow")
    order = hamiltonian_tiles.shape[0]
    rows, width = start_vectors.shape
    assert rows * narrow == order
    routes = Routes(wide, narrow)
    cuts = routes.cuts
    n = rows // cuts
    slots = ITERS if narrow <= 4 else 1
    sequence = steps_of(routes)
    if len(ORDER) == len(sequence):
        sequence = [sequence[place] for place in ORDER]
    copies = sends_of(routes)
    wholes, halves = max(1, len(routes.whole)), max(1, len(routes.half))
    f32, bf16 = jnp.float32, jnp.bfloat16
    stage_rows = order // LOAD_CHUNKS
    slice_rows = width // wide

    def vmem(*shape, dtype=f32):
        return pltpu.VMEM(shape, dtype)

    return pl.pallas_call(
        functools.partial(kernel, routes, sequence, slots),
        out_shape=jax.ShapeDtypeStruct((rows, width), f32),
        in_specs=[
            pl.BlockSpec(memory_space=pltpu.SMEM),
            pl.BlockSpec(memory_space=pl.ANY),
            pl.BlockSpec(memory_space=pl.ANY),
        ],
        out_specs=pl.BlockSpec(memory_space=pltpu.VMEM),
        scratch_shapes=[
            vmem(rows, width),
            vmem(2, stage_rows, order),
            vmem(order, order, dtype=bf16),
            vmem(order, order, dtype=bf16),
            vmem(order, order, dtype=bf16),
            vmem(order, order, dtype=bf16),
            vmem(SHARES, order, width, dtype=bf16),
            vmem(SHARES, order, width, dtype=bf16),
            vmem(slots, narrow, cuts, n, width),
            vmem(narrow, cuts, n, width),
            vmem(slots, wholes, wide, n, width),
            vmem(slots, halves, wide // 2, n, width),
            vmem(slots, wholes, n, width),
            vmem(slots, wholes, n, width),
            vmem(slots, wholes, n, width),
            vmem(slots, halves, n, width),
            vmem(slots, halves, n, width),
            vmem(slots, wholes, wide, n, width),
            vmem(slots, halves, wide // 2, n, width),
            vmem(slots, wholes, wide, n, width),
            vmem(slots, halves, wide // 2, n, width),
            vmem(slots, halves, n, width),
            vmem(slots, wholes, n, width),
            vmem(slots, narrow - 1, cuts, n, width),
            vmem(slots, narrow - 1, cuts, n, width),
            vmem(cuts, n, width),
            vmem(rows, width),
            vmem(8, 128, dtype=jnp.int32),
            vmem(2, 8, 128, dtype=jnp.int32),
            vmem(ITERS, width, width),
            vmem(ITERS, wide, slice_rows, width),
            vmem(ITERS, slice_rows, width),
            vmem(ITERS, narrow, slice_rows, width),
            vmem(ITERS, slice_rows, width),
            vmem(ITERS, width, width),
            vmem(3, width, width),
            vmem(ITERS, width, width),
            pltpu.SemaphoreType.DMA((2,)),
            pltpu.SemaphoreType.DMA,
            pltpu.SemaphoreType.DMA((copies,)),
            pltpu.SemaphoreType.DMA((copies,)),
            pltpu.SemaphoreType.REGULAR,
        ],
        compiler_params=pltpu.CompilerParams(
            collective_id=0, has_side_effects=True, vmem_limit_bytes=67043328
        ),
    )(row_columns, hamiltonian_tiles, start_vectors)


def solution(mesh):
    return jax.shard_map(
        on_device,
        mesh=mesh,
        in_specs=(P("wide", "narrow"), P("wide", None), P(("wide", "narrow"), None)),
        out_specs=P(("wide", "narrow"), None),
        check_vma=False,
    )
```

```python
import functools

import jax
import jax.numpy as jnp
from jax import lax
from jax.experimental import pallas as pl
from jax.experimental.pallas import tpu as pltpu
from jax.sharding import PartitionSpec as P

ITERS = 2
NS_STEPS = 5
HIGHEST = lax.Precision.HIGHEST
MESH = pl.DeviceIdType.MESH
LOAD_CHUNKS = 12
ORDER = (
    12, 15, 14, 13, 137, 0, 1, 2, 3, 4, 28, 30, 29, 20, 5, 31, 6, 7, 8, 40, 23, 9, 41, 32,
    22, 39, 19, 21, 16, 24, 18, 46, 10, 35, 42, 27, 17, 11, 26, 45, 47, 25, 55, 59, 43, 57, 56, 72,
    58, 60, 63, 51, 33, 44, 70, 34, 62, 48, 64, 68, 50, 37, 49, 36, 38, 65, 92, 53, 52, 54, 90, 91,
    93, 108, 76, 96, 74, 101, 106, 107, 66, 112, 69, 100, 71, 77, 97, 80, 61, 75, 73, 67, 83, 95, 82, 79,
    81, 78, 84, 85, 86, 120, 111, 117, 98, 109, 118, 102, 88, 128, 99, 119, 87, 124, 126, 105, 104, 94, 110, 103,
    121, 125, 113, 123, 127, 116, 122, 89, 115, 114, 129, 138, 133, 132, 141, 131, 140, 130, 139, 157, 154, 136, 135, 156,
    146, 155, 149, 165, 148, 158, 168, 147, 166, 161, 143, 173, 134, 243, 177, 171, 150, 160, 144, 170, 199, 167, 152, 169,
    153, 176, 142, 145, 151, 181, 184, 185, 182, 183, 190, 193, 172, 186, 189, 163, 191, 164, 159, 188, 179, 162, 200, 180,
    174, 204, 175, 192, 218, 178, 217, 234, 219, 203, 196, 198, 195, 233, 221, 206, 207, 216, 222, 187, 244, 197, 210, 227,
    225, 232, 194, 238, 201, 202, 205, 208, 211, 209, 212, 254, 214, 237, 253, 224, 251, 220, 226, 230, 252, 236, 235, 213,
    258, 229, 231, 261, 223, 228, 257, 259, 255, 245, 262, 240, 256, 241, 215, 260, 239, 242, 246, 247, 248, 249, 250, 266,
    263, 265, 267, 270, 269, 264, 268, 271, 272, 273, 274, 275, 276, 277, 278,
)


def flip(x, mask):
    bit = 1
    while bit <= mask:
        if mask & bit:
            x = x + bit * (1 - 2 * ((x // bit) % 2))
        bit *= 2
    return x


def bits_of(count):
    bits = count.bit_length() - 1
    assert count == 1 << bits
    return bits


def position(relative, order):
    return sum(((relative >> bit) & 1) << place for place, bit in enumerate(order))


class Routes:
    def __init__(self, wide, narrow):
        self.wide, self.narrow = wide, narrow
        self.wbits, self.nbits = bits_of(wide), bits_of(narrow)
        self.cuts = max(1, 4 * 4 // narrow)
        upper = list(range(1, self.wbits))
        self.lines = [upper, upper[::-1]]
        self.whole = []
        self.half = []
        for q in range(narrow):
            for c in range(self.cuts):
                if self.paired(q, c):
                    if q % 2 == 0:
                        self.whole.append((q, c))
                else:
                    self.half.append((q, c))

    def side(self, q, c):
        return (q + c) % 2

    def paired(self, q, c):
        return q < 2 or c == 0

    def order(self, q, c):
        line = self.lines[self.side(q, c)]
        return line + [0] if self.paired(q, c) else line[:-1] + [0]

    def last(self, q, c):
        return self.lines[self.side(q, c)][-1]

    def straight(self, c):
        return False

    def parent(self, q, c):
        return 0 if self.straight(c) else q & (q - 1)

    def children(self, q, c):
        return [other for other in range(self.narrow - 1, 0, -1) if self.parent(other, c) == q]


def steps_of(routes):
    quarters, cuts = range(routes.narrow), range(routes.cuts)
    steps = [("load", i) for i in range(LOAD_CHUNKS)]
    for it in range(ITERS):
        if it > 0:
            steps.append(("turn", it))
        for q in quarters:
            for c in cuts:
                steps.append(("have", it, q, c))
        for level in range(1, routes.wbits):
            for q in quarters:
                for c in cuts:
                    paired = routes.paired(q, c)
                    if paired and q % 2 == 1:
                        continue
                    if level < len(routes.order(q, c)):
                        steps.append(("step", it, q, c, level))
        for q in quarters:
            for c in cuts:
                if not (routes.paired(q, c) and q % 2 == 1):
                    steps.append(("pick", it, q, c))
        for q in quarters[::-1]:
            steps.append(("trans", it, q))
            for c in cuts:
                if not (routes.paired(q, c) and q % 2 == 0):
                    steps.append(("pass", it, q, c))
        for q in quarters:
            for c in cuts:
                steps.append(("column", it, q, c))
        for q in quarters[::-1]:
            steps.append(("direct", it, q))
        for q in quarters[::-1]:
            for c in cuts:
                if not (routes.paired(q, c) and q % 2 == 1):
                    steps.append(("put", it, q, c))
        for level in range(routes.wbits - 1, 0, -1):
            for q in quarters[::-1]:
                for c in cuts:
                    if routes.paired(q, c) and q % 2 == 1:
                        continue
                    if level < len(routes.order(q, c)):
                        steps.append(("down", it, q, c, level))
        if it > 0:
            steps.append(("spread", it - 1))
            steps.append(("sum", it - 1))
            steps.append(("all", it - 1))
            steps += [("root", it - 1, repeat) for repeat in range(NS_STEPS)]
        for q in quarters[::-1]:
            for c in cuts:
                steps.append(("merge", it, q, c))
        for c in cuts:
            steps.append(("gram", it, c))
    steps.append(("spread", ITERS - 1))
    steps.append(("sum", ITERS - 1))
    steps.append(("all", ITERS - 1))
    steps += [("root", ITERS - 1, repeat) for repeat in range(NS_STEPS)]
    return steps


def sends_of(routes):
    count = 2
    pieces = routes.narrow * routes.cuts
    for it in range(ITERS):
        count += 2 * (routes.narrow - 1) * routes.cuts
        count += 2 * len(routes.whole) * (routes.wbits + 1)
        count += 2 * len(routes.half) * routes.wbits
        count += 2 * (routes.wide - 1) + routes.narrow - 1
    return count


def split(x):
    high = x.astype(jnp.bfloat16)
    low = (x - high.astype(jnp.float32)).astype(jnp.bfloat16)
    return high, low


def split_dot(a, b):
    a_high, a_low = split(a)
    b_high, b_low = split(b)
    left = jnp.concatenate([a_high, a_low], axis=1)
    right = jnp.concatenate(
        [jnp.concatenate([b_high, b_low], axis=1), jnp.concatenate([b_high, jnp.zeros_like(b_low)], axis=1)], axis=0
    )
    both = jnp.dot(left, right, preferred_element_type=jnp.float32)
    return both[:, : b.shape[1]] + both[:, b.shape[1]:]


def tree_sum(values):
    while len(values) > 1:
        values = [a + b for a, b in zip(values[::2], values[1::2])]
    return values[0]


def kernel(routes, sequence, slots, row_columns, tile_hbm, start_hbm, out, start, stage, tile_hi, tile_lo, turn_hi, turn_lo,
           rows_right, columns_right, trans, direct, whole_in, half_in, mate_rows, picks, picked, choices, chosen,
           whole_put, half_put, whole_back, half_back, passed, passed_mate, part, part_in, product, want, wants,
           grams, gram_in, gram_sum, gram_near, gram_part, gram_all, ns, roots,
           stage_sem, start_sem, send_sem, recv_sem, fence_sem):
    wide, narrow, cuts = routes.wide, routes.narrow, routes.cuts
    me_w = lax.axis_index("wide")
    me_z = lax.axis_index("narrow")
    order = tile_hi.shape[0]
    rows, width = start.shape
    n = rows // cuts
    wbits = routes.wbits
    f32 = jnp.float32
    slice_rows = width // wide
    total_rows = float(wide * order)
    whole_at = {unit: place for place, unit in enumerate(routes.whole)}
    half_at = {unit: place for place, unit in enumerate(routes.half)}

    def wide_peer(mask):
        return {"wide": flip(me_w, mask), "narrow": me_z}

    def near_peer(mask):
        return {"wide": me_w, "narrow": flip(me_z, mask)}

    peers = [wide_peer(m) for m in range(1, wide)] + [near_peer(m) for m in range(1, narrow)]
    barrier = pltpu.get_barrier_semaphore()
    for peer in peers:
        pl.semaphore_signal(barrier, inc=1, device_id=peer, device_id_type=MESH)

    stage_rows = stage.shape[1]
    stages = stage.shape[0]

    def fetch(chunk):
        return pltpu.make_async_copy(
            tile_hbm.at[pl.ds(chunk * stage_rows, stage_rows)],
            stage.at[chunk % stages],
            stage_sem.at[chunk % stages],
        )

    begin = pltpu.make_async_copy(start_hbm, start, start_sem)
    begin.start()
    for chunk in range(stages):
        fetch(chunk).start()

    mate = flip(me_z, 1)
    own_want = row_columns[0, me_z] ^ me_w
    mate_want = row_columns[0, mate] ^ me_w
    want[...] = jnp.full(want.shape, own_want, jnp.int32)
    pl.semaphore_wait(barrier, len(peers))

    sent = {}
    waited = set()

    def send(name, source, target, peer):
        index = len(sent)
        copy = pltpu.make_async_remote_copy(
            src_ref=source, dst_ref=target, send_sem=send_sem.at[index], recv_sem=recv_sem.at[index],
            device_id=peer, device_id_type=MESH,
        )
        copy.start()
        assert name not in sent
        sent[name] = copy

    def received(name):
        sent[name].wait_recv()

    def all_gone(*spared):
        for name, copy in sent.items():
            if name not in waited and name[0] not in spared:
                copy.wait_send()
                waited.add(name)

    begin.wait()
    for side in range(2):
        send(("want", side), want, wants.at[side], wide_peer(1 << routes.lines[side][-1]))
    wants_here = set()

    def natural(q):
        return pl.multiple_of(flip(me_z, q) * rows, rows)

    def piece_at(q, c):
        return pl.ds(pl.multiple_of(natural(q) + c * n, n), n)

    def here(it):
        return it % slots

    def gathered(it, q, c):
        if routes.paired(q, c):
            return whole_in.at[here(it), whole_at[q, c]]
        return half_in.at[here(it), half_at[q, c]]

    def row_ref(it, q, c):
        if routes.paired(q, c) and q % 2 == 1:
            return mate_rows.at[here(it), whole_at[q - 1, c]]
        return gathered(it, q, c).at[0]

    def put_ref(it, q, c):
        if routes.paired(q, c):
            return whole_put.at[here(it), whole_at[q, c]]
        return half_put.at[here(it), half_at[q, c]]

    def back_ref(it, q, c):
        if routes.paired(q, c):
            return whole_back.at[here(it), whole_at[q, c]]
        return half_back.at[here(it), half_at[q, c]]

    def keep_split(target, at, value):
        hi, lo = split(value)
        target[at, pl.ds(0, width)] = hi
        target[at, pl.ds(width, width)] = lo

    def far_codes(q, c):
        side = routes.side(q, c)
        if side not in wants_here:
            received(("want", side))
            wants_here.add(side)
        code = wants[side, pl.ds(0, 1), :]
        place = position(code, routes.order(q, c))
        place = jnp.where((code >> routes.last(q, c)) & 1 == 1, place, wide)
        return jnp.broadcast_to(place, (n, width))

    def choose(ref, count, place):
        value = ref[0]
        for p in range(1, count):
            value = jnp.where(place == p, ref[p], value)
        return value

    def start_step(it, q, c, level):
        ref = gathered(it, q, c)
        count = 1 << level
        send(
            ("gather", it, q, c, level), ref.at[pl.ds(0, count)], ref.at[pl.ds(count, count)],
            wide_peer(1 << routes.order(q, c)[level]),
        )

    def start_back(it, q, c, level):
        count = 1 << level
        send(
            ("back", it, q, c, level), put_ref(it, q, c).at[pl.ds(count, count)],
            back_ref(it, q, c).at[pl.ds(count, count)], wide_peer(1 << routes.order(q, c)[level]),
        )

    def do_load(chunk):
        fetch(chunk).wait()
        hi, lo = split(stage[chunk % stages])
        at = pl.ds(chunk * stage_rows, stage_rows)
        tile_hi[at, :] = hi
        tile_lo[at, :] = lo
        turn_hi[:, at] = hi.T
        turn_lo[:, at] = lo.T
        if chunk + stages < LOAD_CHUNKS:
            fetch(chunk + stages).start()

    def do_turn(it):
        if slots == ITERS:
            return
        all_gone()
        for peer in peers:
            pl.semaphore_signal(fence_sem, inc=1, device_id=peer, device_id_type=MESH)
        pl.semaphore_wait(fence_sem, len(peers))
        for c in range(cuts):
            row_ref(it, 0, c)[...] = product[pl.ds(c * n, n), :]

    def do_have(it, q, c):
        ref = row_ref(it, q, c)
        if q > 0:
            received(("rows", it, q, c))
        elif it == 0:
            ref[...] = start[pl.ds(c * n, n), :]
        for child in routes.children(q, c):
            send(("rows", it, child, c), ref, row_ref(it, child, c), near_peer(child ^ q))
        if not (routes.paired(q, c) and q % 2 == 1):
            start_step(it, q, c, 0)
        keep_split(rows_right, piece_at(q, c), ref[...])

    def do_step(it, q, c, level):
        received(("gather", it, q, c, level - 1))
        start_step(it, q, c, level)

    def do_pick(it, q, c):
        levels = len(routes.order(q, c))
        received(("gather", it, q, c, levels - 1))
        if routes.paired(q, c):
            at = whole_at[q, c]
            picks[here(it), at] = choose(gathered(it, q, c), wide, position(mate_want, routes.order(q, c)))
            send(("pick", it, q, c), picks.at[here(it), at], picked.at[here(it), at], near_peer(1))
        else:
            at = half_at[q, c]
            choices[here(it), at] = choose(gathered(it, q, c), wide // 2, far_codes(q, c))
            send(
                ("pick", it, q, c), choices.at[here(it), at], chosen.at[here(it), at],
                wide_peer(1 << routes.last(q, c)),
            )

    def do_column(it, q, c):
        if routes.paired(q, c):
            if q % 2 == 0:
                value = choose(gathered(it, q, c), wide, position(own_want, routes.order(q, c)))
            else:
                received(("pick", it, q - 1, c))
                value = picked[here(it), whole_at[q - 1, c]]
        else:
            received(("pick", it, q, c))
            value = choose(gathered(it, q, c), wide // 2, position(own_want, routes.order(q, c)))
            value = jnp.where((own_want >> routes.last(q, c)) & 1 == 1, chosen[here(it), half_at[q, c]], value)
        keep_split(columns_right, piece_at(q, c), value)

    def product_of(hi, lo, right, at):
        both = jnp.dot(hi[at, :], right[...], preferred_element_type=f32)
        rest = jnp.dot(lo[at, :], right[:, pl.ds(0, width)], preferred_element_type=f32)
        return both[:, :width] + (both[:, width:] + rest)

    def do_trans(it, q):
        at = pl.ds(natural(q), rows)
        trans[here(it), at, :] = product_of(turn_hi, turn_lo, rows_right, at)

    def do_direct(it, q):
        at = pl.ds(natural(q), rows)
        direct[at, :] = product_of(tile_hi, tile_lo, columns_right, at)

    def do_pass(it, q, c):
        source = trans.at[here(it), piece_at(q, c)]
        if routes.paired(q, c):
            send(("pass", it, q, c), source, passed_mate.at[here(it), whole_at[q - 1, c]], near_peer(1))
        else:
            send(
                ("pass", it, q, c), source, passed.at[here(it), half_at[q, c]],
                wide_peer(1 << routes.last(q, c)),
            )

    def do_put(it, q, c):
        mine = trans[here(it), piece_at(q, c), :]
        ref = put_ref(it, q, c)
        places = routes.order(q, c)
        if routes.paired(q, c):
            received(("pass", it, q + 1, c))
            other = passed_mate[here(it), whole_at[q, c]]
            count, first, second = wide, position(own_want, places), position(mate_want, places)
        else:
            received(("pass", it, q, c))
            other = passed[here(it), half_at[q, c]]
            count, second = wide // 2, far_codes(q, c)
            first = position(own_want, places) + wide * ((own_want >> routes.last(q, c)) & 1)
        for p in range(count):
            ref[p] = jnp.where(first == p, mine, 0.0) + jnp.where(second == p, other, 0.0)
        start_back(it, q, c, len(places) - 1)

    def do_down(it, q, c, level):
        received(("back", it, q, c, level))
        count = 1 << level
        ref, came = put_ref(it, q, c), back_ref(it, q, c)
        for p in range(count):
            ref[p] = ref[p] + came[count + p]
        start_back(it, q, c, level - 1)

    def do_merge(it, q, c):
        value = direct[piece_at(q, c), :]
        if not (routes.paired(q, c) and q % 2 == 1):
            received(("back", it, q, c, 0))
            value = value + (put_ref(it, q, c)[0] + back_ref(it, q, c)[1])
        for child in routes.children(q, c):
            received(("part", it, child, c))
            value = value + part_in[here(it), child - 1, c]
        if q > 0:
            part[here(it), q - 1, c] = value
            send(("part", it, q, c), part.at[here(it), q - 1, c], part_in.at[here(it), q - 1, c],
                 near_peer(q ^ routes.parent(q, c)))
        elif it < ITERS - 1:
            product[pl.ds(c * n, n), :] = value
            if slots == ITERS:
                row_ref(it + 1, 0, c)[...] = value
        else:
            product[pl.ds(c * n, n), :] = split_dot(value, roots[it - 1])

    grams_begun = set()

    def do_gram(it, c):
        value = product[pl.ds(c * n, n), :]
        square = lax.dot_general(value, value, (((0,), (0,)), ((), ())), precision=HIGHEST, preferred_element_type=f32)
        if it in grams_begun:
            grams[it] = grams[it] + square
        else:
            grams[it] = square
        grams_begun.add(it)

    def slice_of(mask):
        return pl.ds(pl.multiple_of(flip(me_w, mask) * slice_rows, slice_rows), slice_rows)

    def do_spread(it):
        for mask in range(1, wide):
            send(("spread", it, mask), grams.at[it, slice_of(mask)], gram_in.at[it, mask], wide_peer(mask))

    def do_sum(it):
        if it == ITERS - 1:
            all_gone("spread")
        values = [grams[it, slice_of(0), :]]
        for mask in range(1, wide):
            received(("spread", it, mask))
            values.append(gram_in[it, mask])
        gram_sum[it] = tree_sum(values)
        for mask in range(1, narrow):
            send(("near", it, mask), gram_sum.at[it], gram_near.at[it, mask], near_peer(mask))

    def do_all(it):
        if it == ITERS - 1:
            all_gone("near")
        values = [gram_sum[it]]
        for mask in range(1, narrow):
            received(("near", it, mask))
            values.append(gram_near[it, mask])
        gram_part[it] = tree_sum(values)
        for mask in range(1, wide):
            send(("all", it, mask), gram_part.at[it], gram_all.at[it, slice_of(0)], wide_peer(mask))
        gram_all[it, slice_of(0), :] = gram_part[it]

    def identity():
        row = lax.broadcasted_iota(jnp.int32, (width, width), 0)
        column = lax.broadcasted_iota(jnp.int32, (width, width), 1)
        return jnp.where(row == column, 1.0, 0.0).astype(f32)

    def do_root(it, repeat):
        if repeat == 0:
            if it == ITERS - 1:
                all_gone("all")
            for mask in range(1, wide):
                received(("all", it, mask))
            gram = gram_all[it]
            square = jnp.sum(gram * gram, axis=1, keepdims=True)
            scale = jnp.sqrt(jnp.sum(square, axis=0, keepdims=True) + 1e-06)
            current = gram / scale
            middle = 1.5 * identity() - 0.5 * current
            inverse = middle
            ns[2] = jnp.broadcast_to(jnp.sqrt(total_rows / scale), (width, width))
        else:
            current, inverse = ns[0], ns[1]
            middle = 1.5 * identity() - 0.5 * split_dot(inverse, current)
            inverse = split_dot(middle, inverse)
        if repeat < NS_STEPS - 1:
            ns[0] = split_dot(current, middle)
            ns[1] = inverse
        else:
            roots[it] = inverse * ns[2]

    actions = dict(
        load=do_load, turn=do_turn, have=do_have, step=do_step, pick=do_pick, column=do_column, trans=do_trans,
        direct=do_direct, put=do_put, down=do_down, merge=do_merge, gram=do_gram, spread=do_spread, sum=do_sum,
        all=do_all, root=do_root,
    )
    actions["pass"] = do_pass
    for name in sequence:
        actions[name[0]](*name[1:])
    all_gone()
    out[...] = split_dot(product[...], roots[ITERS - 1])


def on_device(hamiltonian_tiles, row_columns, start_vectors):
    wide, narrow = lax.axis_size("wide"), lax.axis_size("narrow")
    order = hamiltonian_tiles.shape[0]
    rows, width = start_vectors.shape
    assert rows * narrow == order
    routes = Routes(wide, narrow)
    cuts = routes.cuts
    n = rows // cuts
    slots = ITERS if narrow <= 4 else 1
    sequence = steps_of(routes)
    if len(ORDER) == len(sequence):
        sequence = [sequence[place] for place in ORDER]
    copies = sends_of(routes)
    wholes, halves = max(1, len(routes.whole)), max(1, len(routes.half))
    f32, bf16 = jnp.float32, jnp.bfloat16
    stage_rows = order // LOAD_CHUNKS
    slice_rows = width // wide

    def vmem(*shape, dtype=f32):
        return pltpu.VMEM(shape, dtype)

    return pl.pallas_call(
        functools.partial(kernel, routes, sequence, slots),
        out_shape=jax.ShapeDtypeStruct((rows, width), f32),
        in_specs=[
            pl.BlockSpec(memory_space=pltpu.SMEM),
            pl.BlockSpec(memory_space=pl.ANY),
            pl.BlockSpec(memory_space=pl.ANY),
        ],
        out_specs=pl.BlockSpec(memory_space=pltpu.VMEM),
        scratch_shapes=[
            vmem(rows, width),
            vmem(2, stage_rows, order),
            vmem(order, order, dtype=bf16),
            vmem(order, order, dtype=bf16),
            vmem(order, order, dtype=bf16),
            vmem(order, order, dtype=bf16),
            vmem(order, 2 * width, dtype=bf16),
            vmem(order, 2 * width, dtype=bf16),
            vmem(slots, order, width),
            vmem(order, width),
            vmem(slots, wholes, wide, n, width),
            vmem(slots, halves, wide // 2, n, width),
            vmem(slots, wholes, n, width),
            vmem(slots, wholes, n, width),
            vmem(slots, wholes, n, width),
            vmem(slots, halves, n, width),
            vmem(slots, halves, n, width),
            vmem(slots, wholes, wide, n, width),
            vmem(slots, halves, wide // 2, n, width),
            vmem(slots, wholes, wide, n, width),
            vmem(slots, halves, wide // 2, n, width),
            vmem(slots, halves, n, width),
            vmem(slots, wholes, n, width),
            vmem(slots, narrow - 1, cuts, n, width),
            vmem(slots, narrow - 1, cuts, n, width),
            vmem(rows, width),
            vmem(8, 128, dtype=jnp.int32),
            vmem(2, 8, 128, dtype=jnp.int32),
            vmem(ITERS, width, width),
            vmem(ITERS, wide, slice_rows, width),
            vmem(ITERS, slice_rows, width),
            vmem(ITERS, narrow, slice_rows, width),
            vmem(ITERS, slice_rows, width),
            vmem(ITERS, width, width),
            vmem(3, width, width),
            vmem(ITERS, width, width),
            pltpu.SemaphoreType.DMA((2,)),
            pltpu.SemaphoreType.DMA,
            pltpu.SemaphoreType.DMA((copies,)),
            pltpu.SemaphoreType.DMA((copies,)),
            pltpu.SemaphoreType.REGULAR,
        ],
        compiler_params=pltpu.CompilerParams(
            collective_id=0, has_side_effects=True, vmem_limit_bytes=67043328
        ),
    )(row_columns, hamiltonian_tiles, start_vectors)


def solution(mesh):
    return jax.shard_map(
        on_device,
        mesh=mesh,
        in_specs=(P("wide", "narrow"), P("wide", None), P(("wide", "narrow"), None)),
        out_specs=P(("wide", "narrow"), None),
        check_vma=False,
    )
```

```python
import functools

import jax
import jax.numpy as jnp
from jax import lax
from jax.experimental import pallas as pl
from jax.experimental.pallas import tpu as pltpu
from jax.sharding import PartitionSpec as P

ITERS = 2
NS_STEPS = 5
HIGHEST = lax.Precision.HIGHEST
MESH = pl.DeviceIdType.MESH
LOAD_CHUNKS = 12
ORDER = (
    13, 14, 0, 1, 2, 15, 3, 12, 4, 30, 29, 21, 31, 5, 6, 7, 22, 8, 9, 23, 10, 28, 40, 42,
    20, 33, 72, 44, 16, 11, 41, 18, 35, 19, 25, 17, 34, 54, 26, 48, 27, 45, 39, 50, 32, 24, 55, 58,
    59, 74, 57, 47, 46, 56, 49, 38, 37, 76, 60, 64, 65, 69, 80, 36, 53, 82, 43, 73, 86, 93, 67, 92,
    52, 51, 78, 108, 91, 68, 62, 97, 77, 66, 61, 107, 79, 70, 101, 85, 106, 81, 75, 71, 84, 83, 87, 120,
    112, 95, 99, 63, 105, 119, 88, 98, 118, 117, 94, 103, 110, 89, 100, 124, 109, 137, 102, 96, 125, 126, 122, 116,
    104, 111, 128, 121, 113, 114, 127, 123, 90, 132, 141, 115, 130, 139, 134, 129, 138, 157, 131, 140, 135, 133, 155, 149,
    154, 147, 168, 136, 161, 156, 146, 148, 180, 166, 176, 144, 243, 165, 170, 172, 145, 159, 142, 143, 158, 198, 167, 151,
    153, 200, 150, 160, 174, 169, 152, 181, 182, 183, 184, 191, 193, 173, 186, 190, 162, 194, 202, 163, 171, 204, 175, 197,
    164, 208, 177, 178, 217, 179, 185, 187, 192, 218, 196, 225, 201, 219, 223, 212, 232, 188, 189, 205, 244, 233, 199, 229,
    209, 207, 226, 195, 210, 203, 234, 206, 211, 213, 254, 238, 215, 262, 230, 220, 251, 235, 252, 221, 227, 214, 245, 258,
    236, 222, 231, 224, 253, 237, 228, 255, 261, 256, 241, 260, 246, 242, 216, 257, 240, 239, 247, 259, 248, 249, 250, 266,
    270, 264, 268, 265, 269, 263, 267, 271, 272, 273, 274, 275, 276, 277, 278,
)


def flip(x, mask):
    bit = 1
    while bit <= mask:
        if mask & bit:
            x = x + bit * (1 - 2 * ((x // bit) % 2))
        bit *= 2
    return x


def bits_of(count):
    bits = count.bit_length() - 1
    assert count == 1 << bits
    return bits


def position(relative, order):
    return sum(((relative >> bit) & 1) << place for place, bit in enumerate(order))


class Routes:
    def __init__(self, wide, narrow):
        self.wide, self.narrow = wide, narrow
        self.wbits, self.nbits = bits_of(wide), bits_of(narrow)
        self.cuts = max(1, 4 * 4 // narrow)
        upper = list(range(1, self.wbits))
        self.lines = [upper, upper[::-1]]
        pieces = [(q, c) for q in range(narrow) for c in range(self.cuts)]
        self.whole = [(q, c) for q, c in pieces if q == 0]
        self.given = [(q, c) for q, c in pieces if self.served(q, c)]
        self.half = [(q, c) for q, c in pieces if q > 0 and not self.served(q, c)]

    def side(self, q, c):
        return (q + c) % 2

    def served(self, q, c):
        return q > 0 and (q == 1 or (q == 3 and c == 3))

    def order(self, q, c):
        line = self.lines[self.side(q, c)]
        return line + [0] if q == 0 else line[:-1] + [0]

    def last(self, q, c):
        return self.lines[self.side(q, c)][-1]

    def straight(self, c):
        return False

    def parent(self, q, c):
        return 0 if self.straight(c) else q & (q - 1)

    def children(self, q, c):
        return [other for other in range(self.narrow - 1, 0, -1) if self.parent(other, c) == q]


def steps_of(routes):
    quarters, cuts = range(routes.narrow), range(routes.cuts)
    steps = [("load", i) for i in range(LOAD_CHUNKS)]
    for it in range(ITERS):
        if it > 0:
            steps.append(("turn", it))
        for q in quarters:
            for c in cuts:
                steps.append(("have", it, q, c))
        for level in range(1, routes.wbits):
            for q in quarters:
                for c in cuts:
                    if not routes.served(q, c) and level < len(routes.order(q, c)):
                        steps.append(("step", it, q, c, level))
        for q in quarters:
            for c in cuts:
                if q > 0:
                    steps.append(("pick", it, q, c))
        for q in quarters[::-1]:
            steps.append(("trans", it, q))
            for c in cuts:
                if q > 0:
                    steps.append(("pass", it, q, c))
        for q in quarters:
            for c in cuts:
                steps.append(("column", it, q, c))
        for q in quarters[::-1]:
            steps.append(("direct", it, q))
        for q in quarters[::-1]:
            for c in cuts:
                if not routes.served(q, c):
                    steps.append(("put", it, q, c))
        for level in range(routes.wbits - 1, 0, -1):
            for q in quarters[::-1]:
                for c in cuts:
                    if not routes.served(q, c) and level < len(routes.order(q, c)):
                        steps.append(("down", it, q, c, level))
        if it > 0:
            steps.append(("spread", it - 1))
            steps.append(("sum", it - 1))
            steps.append(("all", it - 1))
            steps += [("root", it - 1, repeat) for repeat in range(NS_STEPS)]
        for q in quarters[::-1]:
            for c in cuts:
                steps.append(("merge", it, q, c))
        for c in cuts:
            steps.append(("gram", it, c))
    steps.append(("spread", ITERS - 1))
    steps.append(("sum", ITERS - 1))
    steps.append(("all", ITERS - 1))
    steps += [("root", ITERS - 1, repeat) for repeat in range(NS_STEPS)]
    return steps


def sends_of(routes):
    count = 2
    pieces = routes.narrow * routes.cuts
    for it in range(ITERS):
        count += 2 * (routes.narrow - 1) * routes.cuts
        count += 2 * len(routes.whole) * routes.wbits + 2 * len(routes.given)
        count += 2 * len(routes.half) * routes.wbits
        count += 2 * (routes.wide - 1) + routes.narrow - 1
    return count


def split(x):
    high = x.astype(jnp.bfloat16)
    low = (x - high.astype(jnp.float32)).astype(jnp.bfloat16)
    return high, low


def split_dot(a, b):
    a_high, a_low = split(a)
    b_high, b_low = split(b)
    left = jnp.concatenate([a_high, a_low], axis=1)
    right = jnp.concatenate(
        [jnp.concatenate([b_high, b_low], axis=1), jnp.concatenate([b_high, jnp.zeros_like(b_low)], axis=1)], axis=0
    )
    both = jnp.dot(left, right, preferred_element_type=jnp.float32)
    return both[:, : b.shape[1]] + both[:, b.shape[1]:]


def tree_sum(values):
    while len(values) > 1:
        values = [a + b for a, b in zip(values[::2], values[1::2])]
    return values[0]


def kernel(routes, sequence, slots, row_columns, tile_hbm, start_hbm, out, start, stage, tile_hi, tile_lo, turn_hi, turn_lo,
           rows_right, columns_right, trans, direct, whole_in, half_in, mate_rows, picks, picked, choices, chosen,
           whole_put, half_put, whole_back, half_back, passed, passed_mate, part, part_in, product, want, wants,
           grams, gram_in, gram_sum, gram_near, gram_part, gram_all, ns, roots,
           stage_sem, start_sem, send_sem, recv_sem, fence_sem):
    wide, narrow, cuts = routes.wide, routes.narrow, routes.cuts
    me_w = lax.axis_index("wide")
    me_z = lax.axis_index("narrow")
    order = tile_hi.shape[0]
    rows, width = start.shape
    n = rows // cuts
    wbits = routes.wbits
    f32 = jnp.float32
    slice_rows = width // wide
    total_rows = float(wide * order)
    whole_at = {unit: place for place, unit in enumerate(routes.whole)}
    half_at = {unit: place for place, unit in enumerate(routes.half)}
    given_at = {unit: place for place, unit in enumerate(routes.given)}

    def wide_peer(mask):
        return {"wide": flip(me_w, mask), "narrow": me_z}

    def near_peer(mask):
        return {"wide": me_w, "narrow": flip(me_z, mask)}

    peers = [wide_peer(m) for m in range(1, wide)] + [near_peer(m) for m in range(1, narrow)]
    barrier = pltpu.get_barrier_semaphore()
    for peer in peers:
        pl.semaphore_signal(barrier, inc=1, device_id=peer, device_id_type=MESH)

    stage_rows = stage.shape[1]
    stages = stage.shape[0]

    def fetch(chunk):
        return pltpu.make_async_copy(
            tile_hbm.at[pl.ds(chunk * stage_rows, stage_rows)],
            stage.at[chunk % stages],
            stage_sem.at[chunk % stages],
        )

    begin = pltpu.make_async_copy(start_hbm, start, start_sem)
    begin.start()
    for chunk in range(stages):
        fetch(chunk).start()

    near_wants = [row_columns[0, flip(me_z, q)] ^ me_w for q in range(narrow)]
    own_want = near_wants[0]
    want[...] = jnp.full(want.shape, own_want, jnp.int32)
    pl.semaphore_wait(barrier, len(peers))

    sent = {}
    waited = set()

    def send(name, source, target, peer):
        index = len(sent)
        copy = pltpu.make_async_remote_copy(
            src_ref=source, dst_ref=target, send_sem=send_sem.at[index], recv_sem=recv_sem.at[index],
            device_id=peer, device_id_type=MESH,
        )
        copy.start()
        assert name not in sent
        sent[name] = copy

    def received(name):
        sent[name].wait_recv()

    def all_gone(*spared):
        for name, copy in sent.items():
            if name not in waited and name[0] not in spared:
                copy.wait_send()
                waited.add(name)

    begin.wait()
    for side in range(2):
        send(("want", side), want, wants.at[side], wide_peer(1 << routes.lines[side][-1]))
    wants_here = set()

    def natural(q):
        return pl.multiple_of(flip(me_z, q) * rows, rows)

    def piece_at(q, c):
        return pl.ds(pl.multiple_of(natural(q) + c * n, n), n)

    def here(it):
        return it % slots

    def gathered(it, q, c):
        if q == 0:
            return whole_in.at[here(it), whole_at[q, c]]
        return half_in.at[here(it), half_at[q, c]]

    def row_ref(it, q, c):
        if routes.served(q, c):
            return mate_rows.at[here(it), given_at[q, c]]
        return gathered(it, q, c).at[0]

    def put_ref(it, q, c):
        if q == 0:
            return whole_put.at[here(it), whole_at[q, c]]
        return half_put.at[here(it), half_at[q, c]]

    def back_ref(it, q, c):
        if q == 0:
            return whole_back.at[here(it), whole_at[q, c]]
        return half_back.at[here(it), half_at[q, c]]

    def keep_split(target, at, value):
        hi, lo = split(value)
        target[at, pl.ds(0, width)] = hi
        target[at, pl.ds(width, width)] = lo

    def far_codes(q, c):
        side = routes.side(q, c)
        if side not in wants_here:
            received(("want", side))
            wants_here.add(side)
        code = wants[side, pl.ds(0, 1), :]
        place = position(code, routes.order(q, c))
        place = jnp.where((code >> routes.last(q, c)) & 1 == 1, place, wide)
        return jnp.broadcast_to(place, (n, width))

    def choose(ref, count, place):
        value = ref[0]
        for p in range(1, count):
            value = jnp.where(place == p, ref[p], value)
        return value

    def start_step(it, q, c, level):
        ref = gathered(it, q, c)
        count = 1 << level
        send(
            ("gather", it, q, c, level), ref.at[pl.ds(0, count)], ref.at[pl.ds(count, count)],
            wide_peer(1 << routes.order(q, c)[level]),
        )

    def start_back(it, q, c, level):
        count = 1 << level
        send(
            ("back", it, q, c, level), put_ref(it, q, c).at[pl.ds(count, count)],
            back_ref(it, q, c).at[pl.ds(count, count)], wide_peer(1 << routes.order(q, c)[level]),
        )

    def do_load(chunk):
        fetch(chunk).wait()
        hi, lo = split(stage[chunk % stages])
        at = pl.ds(chunk * stage_rows, stage_rows)
        tile_hi[at, :] = hi
        tile_lo[at, :] = lo
        turn_hi[:, at] = hi.T
        turn_lo[:, at] = lo.T
        if chunk + stages < LOAD_CHUNKS:
            fetch(chunk + stages).start()

    def do_turn(it):
        if slots == ITERS:
            return
        all_gone()
        for peer in peers:
            pl.semaphore_signal(fence_sem, inc=1, device_id=peer, device_id_type=MESH)
        pl.semaphore_wait(fence_sem, len(peers))
        for c in range(cuts):
            row_ref(it, 0, c)[...] = product[pl.ds(c * n, n), :]

    def do_have(it, q, c):
        ref = row_ref(it, q, c)
        if q > 0:
            received(("rows", it, q, c))
        elif it == 0:
            ref[...] = start[pl.ds(c * n, n), :]
        for child in routes.children(q, c):
            send(("rows", it, child, c), ref, row_ref(it, child, c), near_peer(child ^ q))
        if not routes.served(q, c):
            start_step(it, q, c, 0)
        keep_split(rows_right, piece_at(q, c), ref[...])

    def do_step(it, q, c, level):
        received(("gather", it, q, c, level - 1))
        start_step(it, q, c, level)

    complete = set()

    def finish_gather(it, q, c):
        if (it, q, c) not in complete:
            complete.add((it, q, c))
            received(("gather", it, q, c, len(routes.order(q, c)) - 1))

    def do_pick(it, q, c):
        if routes.served(q, c):
            finish_gather(it, 0, c)
            at = given_at[q, c]
            picks[here(it), at] = choose(gathered(it, 0, c), wide, position(near_wants[q], routes.order(0, c)))
            send(("pick", it, q, c), picks.at[here(it), at], picked.at[here(it), at], near_peer(q))
        else:
            finish_gather(it, q, c)
            at = half_at[q, c]
            choices[here(it), at] = choose(gathered(it, q, c), wide // 2, far_codes(q, c))
            send(
                ("pick", it, q, c), choices.at[here(it), at], chosen.at[here(it), at],
                wide_peer(1 << routes.last(q, c)),
            )

    def do_column(it, q, c):
        if q == 0:
            finish_gather(it, q, c)
            value = choose(gathered(it, q, c), wide, position(own_want, routes.order(q, c)))
        elif routes.served(q, c):
            received(("pick", it, q, c))
            value = picked[here(it), given_at[q, c]]
        else:
            finish_gather(it, q, c)
            received(("pick", it, q, c))
            value = choose(gathered(it, q, c), wide // 2, position(own_want, routes.order(q, c)))
            value = jnp.where((own_want >> routes.last(q, c)) & 1 == 1, chosen[here(it), half_at[q, c]], value)
        keep_split(columns_right, piece_at(q, c), value)

    def product_of(hi, lo, right, at):
        both = jnp.dot(hi[at, :], right[...], preferred_element_type=f32)
        rest = jnp.dot(lo[at, :], right[:, pl.ds(0, width)], preferred_element_type=f32)
        return both[:, :width] + (both[:, width:] + rest)

    def do_trans(it, q):
        at = pl.ds(natural(q), rows)
        trans[here(it), at, :] = product_of(turn_hi, turn_lo, rows_right, at)

    def do_direct(it, q):
        at = pl.ds(natural(q), rows)
        direct[at, :] = product_of(tile_hi, tile_lo, columns_right, at)

    def do_pass(it, q, c):
        source = trans.at[here(it), piece_at(q, c)]
        if routes.served(q, c):
            send(("pass", it, q, c), source, passed_mate.at[here(it), given_at[q, c]], near_peer(q))
        else:
            send(
                ("pass", it, q, c), source, passed.at[here(it), half_at[q, c]],
                wide_peer(1 << routes.last(q, c)),
            )

    def do_put(it, q, c):
        mine = trans[here(it), piece_at(q, c), :]
        ref = put_ref(it, q, c)
        places = routes.order(q, c)
        if q == 0:
            count, first = wide, position(own_want, places)
            others = []
            for near in range(1, narrow):
                if routes.served(near, c):
                    received(("pass", it, near, c))
                    others.append((position(near_wants[near], places), passed_mate[here(it), given_at[near, c]]))
        else:
            received(("pass", it, q, c))
            count = wide // 2
            others = [(far_codes(q, c), passed[here(it), half_at[q, c]])]
            first = position(own_want, places) + wide * ((own_want >> routes.last(q, c)) & 1)
        for p in range(count):
            value = jnp.where(first == p, mine, 0.0)
            for place, other in others:
                value = value + jnp.where(place == p, other, 0.0)
            ref[p] = value
        start_back(it, q, c, len(places) - 1)

    def do_down(it, q, c, level):
        received(("back", it, q, c, level))
        count = 1 << level
        ref, came = put_ref(it, q, c), back_ref(it, q, c)
        for p in range(count):
            ref[p] = ref[p] + came[count + p]
        start_back(it, q, c, level - 1)

    def do_merge(it, q, c):
        value = direct[piece_at(q, c), :]
        if not routes.served(q, c):
            received(("back", it, q, c, 0))
            value = value + (put_ref(it, q, c)[0] + back_ref(it, q, c)[1])
        for child in routes.children(q, c):
            received(("part", it, child, c))
            value = value + part_in[here(it), child - 1, c]
        if q > 0:
            part[here(it), q - 1, c] = value
            send(("part", it, q, c), part.at[here(it), q - 1, c], part_in.at[here(it), q - 1, c],
                 near_peer(q ^ routes.parent(q, c)))
        elif it < ITERS - 1:
            product[pl.ds(c * n, n), :] = value
            if slots == ITERS:
                row_ref(it + 1, 0, c)[...] = value
        else:
            product[pl.ds(c * n, n), :] = split_dot(value, roots[it - 1])

    grams_begun = set()

    def do_gram(it, c):
        value = product[pl.ds(c * n, n), :]
        square = lax.dot_general(value, value, (((0,), (0,)), ((), ())), precision=HIGHEST, preferred_element_type=f32)
        if it in grams_begun:
            grams[it] = grams[it] + square
        else:
            grams[it] = square
        grams_begun.add(it)

    def slice_of(mask):
        return pl.ds(pl.multiple_of(flip(me_w, mask) * slice_rows, slice_rows), slice_rows)

    def do_spread(it):
        for mask in range(1, wide):
            send(("spread", it, mask), grams.at[it, slice_of(mask)], gram_in.at[it, mask], wide_peer(mask))

    def do_sum(it):
        if it == ITERS - 1:
            all_gone("spread")
        values = [grams[it, slice_of(0), :]]
        for mask in range(1, wide):
            received(("spread", it, mask))
            values.append(gram_in[it, mask])
        gram_sum[it] = tree_sum(values)
        for mask in range(1, narrow):
            send(("near", it, mask), gram_sum.at[it], gram_near.at[it, mask], near_peer(mask))

    def do_all(it):
        if it == ITERS - 1:
            all_gone("near")
        values = [gram_sum[it]]
        for mask in range(1, narrow):
            received(("near", it, mask))
            values.append(gram_near[it, mask])
        gram_part[it] = tree_sum(values)
        for mask in range(1, wide):
            send(("all", it, mask), gram_part.at[it], gram_all.at[it, slice_of(0)], wide_peer(mask))
        gram_all[it, slice_of(0), :] = gram_part[it]

    def identity():
        row = lax.broadcasted_iota(jnp.int32, (width, width), 0)
        column = lax.broadcasted_iota(jnp.int32, (width, width), 1)
        return jnp.where(row == column, 1.0, 0.0).astype(f32)

    def do_root(it, repeat):
        if repeat == 0:
            if it == ITERS - 1:
                all_gone("all")
            for mask in range(1, wide):
                received(("all", it, mask))
            gram = gram_all[it]
            square = jnp.sum(gram * gram, axis=1, keepdims=True)
            scale = jnp.sqrt(jnp.sum(square, axis=0, keepdims=True) + 1e-06)
            current = gram / scale
            middle = 1.5 * identity() - 0.5 * current
            inverse = middle
            ns[2] = jnp.broadcast_to(jnp.sqrt(total_rows / scale), (width, width))
        else:
            current, inverse = ns[0], ns[1]
            middle = 1.5 * identity() - 0.5 * split_dot(inverse, current)
            inverse = split_dot(middle, inverse)
        if repeat < NS_STEPS - 1:
            ns[0] = split_dot(current, middle)
            ns[1] = inverse
        else:
            roots[it] = inverse * ns[2]

    actions = dict(
        load=do_load, turn=do_turn, have=do_have, step=do_step, pick=do_pick, column=do_column, trans=do_trans,
        direct=do_direct, put=do_put, down=do_down, merge=do_merge, gram=do_gram, spread=do_spread, sum=do_sum,
        all=do_all, root=do_root,
    )
    actions["pass"] = do_pass
    for name in sequence:
        actions[name[0]](*name[1:])
    all_gone()
    out[...] = split_dot(product[...], roots[ITERS - 1])


def on_device(hamiltonian_tiles, row_columns, start_vectors):
    wide, narrow = lax.axis_size("wide"), lax.axis_size("narrow")
    order = hamiltonian_tiles.shape[0]
    rows, width = start_vectors.shape
    assert rows * narrow == order
    routes = Routes(wide, narrow)
    cuts = routes.cuts
    n = rows // cuts
    slots = ITERS if narrow <= 4 else 1
    sequence = steps_of(routes)
    if len(ORDER) == len(sequence):
        sequence = [sequence[place] for place in ORDER]
    copies = sends_of(routes)
    wholes, halves, givens = len(routes.whole), max(1, len(routes.half)), max(1, len(routes.given))
    f32, bf16 = jnp.float32, jnp.bfloat16
    stage_rows = order // LOAD_CHUNKS
    slice_rows = width // wide

    def vmem(*shape, dtype=f32):
        return pltpu.VMEM(shape, dtype)

    return pl.pallas_call(
        functools.partial(kernel, routes, sequence, slots),
        out_shape=jax.ShapeDtypeStruct((rows, width), f32),
        in_specs=[
            pl.BlockSpec(memory_space=pltpu.SMEM),
            pl.BlockSpec(memory_space=pl.ANY),
            pl.BlockSpec(memory_space=pl.ANY),
        ],
        out_specs=pl.BlockSpec(memory_space=pltpu.VMEM),
        scratch_shapes=[
            vmem(rows, width),
            vmem(2, stage_rows, order),
            vmem(order, order, dtype=bf16),
            vmem(order, order, dtype=bf16),
            vmem(order, order, dtype=bf16),
            vmem(order, order, dtype=bf16),
            vmem(order, 2 * width, dtype=bf16),
            vmem(order, 2 * width, dtype=bf16),
            vmem(slots, order, width),
            vmem(order, width),
            vmem(slots, wholes, wide, n, width),
            vmem(slots, halves, wide // 2, n, width),
            vmem(slots, givens, n, width),
            vmem(slots, givens, n, width),
            vmem(slots, givens, n, width),
            vmem(slots, halves, n, width),
            vmem(slots, halves, n, width),
            vmem(slots, wholes, wide, n, width),
            vmem(slots, halves, wide // 2, n, width),
            vmem(slots, wholes, wide, n, width),
            vmem(slots, halves, wide // 2, n, width),
            vmem(slots, halves, n, width),
            vmem(slots, givens, n, width),
            vmem(slots, narrow - 1, cuts, n, width),
            vmem(slots, narrow - 1, cuts, n, width),
            vmem(rows, width),
            vmem(8, 128, dtype=jnp.int32),
            vmem(2, 8, 128, dtype=jnp.int32),
            vmem(ITERS, width, width),
            vmem(ITERS, wide, slice_rows, width),
            vmem(ITERS, slice_rows, width),
            vmem(ITERS, narrow, slice_rows, width),
            vmem(ITERS, slice_rows, width),
            vmem(ITERS, width, width),
            vmem(3, width, width),
            vmem(ITERS, width, width),
            pltpu.SemaphoreType.DMA((2,)),
            pltpu.SemaphoreType.DMA,
            pltpu.SemaphoreType.DMA((copies,)),
            pltpu.SemaphoreType.DMA((copies,)),
            pltpu.SemaphoreType.REGULAR,
        ],
        compiler_params=pltpu.CompilerParams(
            collective_id=0, has_side_effects=True, vmem_limit_bytes=67043328
        ),
    )(row_columns, hamiltonian_tiles, start_vectors)


def solution(mesh):
    return jax.shard_map(
        on_device,
        mesh=mesh,
        in_specs=(P("wide", "narrow"), P("wide", None), P(("wide", "narrow"), None)),
        out_specs=P(("wide", "narrow"), None),
        check_vma=False,
    )
```
